32 devices in a mesh: head: 2 (over y), ctx: 16 (over z, x, core).
Axes of the slice: x: 2, y: 2, z: 4, core: 2. Of those that a mesh axis runs over, the one named last changes fastest.
Arguments:
- queries: bfloat16 [512, 24576], P(None, 'head'), may hold values from -100 to 100
- attn_keys: bfloat16 [4096, 24576], P('ctx', 'head'), may hold values from -6 to 6
- index_queries: bfloat16 [512, 8192], P(None, 'head'), may hold values from -16 to 16
- index_keys: bfloat16 [4096, 128], P('ctx'), may hold values from -6 to 6
- head_weights: float32 [512, 64], P(None, 'head'), may hold values from 0.1 to 1
- query_pos: int32 [512], replicated, may hold values from 16 to 32767
- key_offset: int32 [4096], P('ctx'), may hold values from 0 to 7
Outputs:
- index_query_grad: float32 [512, 8192], P('ctx', 'head')
- index_key_grad: float32 [4096, 128], P('ctx')
The draws below stay inside these ranges and needn't reach their ends.
All inputs are finite; a program needn't handle non-finite values.
Results may differ from the reference program's by a relative error of at most 0.0027.
Values sent between devices are 32-bit elements; how exact they have to be, the bound alone decides.
A program may use at most 128 MiB of HBM per device.

```python
import math
import jax
import jax.numpy as jnp
from jax import lax

HEADS = 128
HEAD_DIM = 192
IHEADS = 64
IDIM = 128
QUERIES = 512
STRIDE = 8
KEYS = 4096


def attn_keys_base(key):
    sub_key = jax.random.fold_in(key, 101)
    base = jnp.clip(jax.random.normal(sub_key, (KEYS, HEADS * HEAD_DIM), jnp.float32), -6.0, 6.0)
    return base


def index_keys_base(key):
    sub_key = jax.random.fold_in(key, 103)
    base = jnp.clip(jax.random.normal(sub_key, (KEYS, IDIM), jnp.float32), -6.0, 6.0)
    return base


def draw_attn_keys(key, part):
    return attn_keys_base(key).astype(jnp.bfloat16)


def draw_index_keys(key, part):
    return index_keys_base(key).astype(jnp.bfloat16)


def draw_queries(key, part):
    sub_key = jax.random.fold_in(key, 102)
    base = jnp.clip(jax.random.normal(sub_key, (QUERIES, HEADS * HEAD_DIM), jnp.float32), -6.0, 6.0)
    return base.astype(jnp.bfloat16)


def draw_index_queries(key, part):
    sub_key = jax.random.fold_in(key, 104)
    base = jnp.clip(jax.random.normal(sub_key, (QUERIES, IHEADS * IDIM), jnp.float32), -6.0, 6.0)
    return base.astype(jnp.bfloat16)


def place_ends(array, key, smallest, high):
    extent = array.shape
    spot = [jax.random.randint(jax.random.fold_in(key, axis), (), 0, extent[axis]) for axis in range(len(extent))]
    array = array.at[tuple(spot)].set(smallest)
    longest = extent.index(max(extent))
    spot[longest] = (spot[longest] + 1) % extent[longest]
    return array.at[tuple(spot)].set(high)


def block_scale(rng, extent, split, smallest, high):
    level = 1.0
    for axis_at, blocks in split:
        draws = jax.random.uniform(jax.random.fold_in(jax.random.fold_in(rng, 6), axis_at), (blocks,), jnp.float32, smallest / len(split), high / len(split))
        level = level * jnp.repeat(jnp.exp(draws), extent[axis_at] // blocks).reshape((-1,) + (1,) * (len(extent) - 1 - axis_at))
    return level


def setup_inputs(seed: int = 0) -> dict:
    streams_of = jax.random.split(jax.random.key(seed), 8)
    return {
        "queries": draw_queries(jax.random.fold_in(streams_of[7], 71), 0),
        "attn_keys": draw_attn_keys(jax.random.fold_in(streams_of[7], 71), 0),
        "index_queries": draw_index_queries(jax.random.fold_in(streams_of[7], 71), 0),
        "index_keys": draw_index_keys(jax.random.fold_in(streams_of[7], 71), 0),
        "head_weights": jnp.clip(jnp.exp(math.log(1.0) - 2.3025851 * jax.random.uniform(streams_of[4], (QUERIES, IHEADS), jnp.float32) ** block_scale(streams_of[4], (QUERIES, IHEADS), ((1, 2),), -0.2, 0.2)), 0.1, 1.0),
        "query_pos": place_ends(jax.random.randint(streams_of[5], (QUERIES,), 2 * STRIDE, STRIDE * KEYS), jax.random.fold_in(streams_of[5], 1), 2 * STRIDE, (STRIDE * KEYS) - 1).astype(jnp.int32),
        "key_offset": place_ends(jax.random.randint(streams_of[6], (KEYS,), 0, STRIDE), jax.random.fold_in(streams_of[6], 1), 0, STRIDE - 1).astype(jnp.int32),
    }


NEG_FILL = -1e+30

def reference(queries, attn_keys, index_queries, index_keys, head_weights, query_pos, key_offset):
    key_pos = STRIDE * jnp.arange(KEYS, dtype=jnp.int32) + key_offset
    visible = key_pos[None, :] <= query_pos[:, None]
    attn_scale = 1.0 / math.sqrt(HEAD_DIM)
    inv_scale = 1.0 / math.sqrt(IDIM)

    def attn_head(total, head_index):
        start = (head_index * HEAD_DIM).astype(jnp.int32)
        query_head = lax.dynamic_slice_in_dim(queries, start, HEAD_DIM, 1)
        key_head = lax.dynamic_slice_in_dim(attn_keys, start, HEAD_DIM, 1)
        scores = jnp.dot(query_head, key_head.T, preferred_element_type=jnp.float32) * attn_scale
        masked = jnp.where(visible, scores, NEG_FILL)
        top_value = lax.optimization_barrier(jnp.max(masked, axis=1, keepdims=True))
        exp_terms = jnp.where(visible, jnp.exp(masked - top_value), 0.0)
        return (total + exp_terms / lax.optimization_barrier(jnp.sum(exp_terms, axis=1, keepdims=True)), None)
    total, _ = lax.scan(attn_head, jnp.zeros((QUERIES, KEYS), jnp.float32), jnp.arange(HEADS, dtype=jnp.int32))
    target = total / HEADS

    def index_slices(head_index):
        start = (head_index * IDIM).astype(jnp.int32)
        query_head = lax.dynamic_slice_in_dim(index_queries, start, IDIM, 1)
        activation = jnp.dot(query_head, index_keys.T, preferred_element_type=jnp.float32) * inv_scale
        weight_col = lax.dynamic_slice_in_dim(head_weights, head_index.astype(jnp.int32), 1, 1)
        return (query_head, activation, weight_col)

    def index_head(logits, head_index):
        query_head, activation, weight_col = index_slices(head_index)
        return (logits + weight_col * jnp.maximum(activation, 0.0), None)
    logits, _ = lax.scan(index_head, jnp.zeros((QUERIES, KEYS), jnp.float32), jnp.arange(IHEADS, dtype=jnp.int32))
    masked = jnp.where(visible, logits, NEG_FILL)
    top_value = lax.optimization_barrier(jnp.max(masked, axis=1, keepdims=True))
    exp_terms = jnp.where(visible, jnp.exp(masked - top_value), 0.0)
    prob_step = exp_terms / lax.optimization_barrier(jnp.sum(exp_terms, axis=1, keepdims=True)) - target

    def grad_head(key_grad, head_index):
        query_head, activation, weight_col = index_slices(head_index)
        grad_terms = jnp.where(activation > 0.0, prob_step * weight_col * inv_scale, 0.0).astype(jnp.bfloat16)
        query_grad = jnp.dot(grad_terms, index_keys, preferred_element_type=jnp.float32)
        key_grad = key_grad + jnp.dot(grad_terms.T, query_head, preferred_element_type=jnp.float32)
        return (key_grad, query_grad)
    key_grad, query_stack = lax.scan(grad_head, jnp.zeros((KEYS, IDIM), jnp.float32), jnp.arange(IHEADS, dtype=jnp.int32))
    query_grad = jnp.transpose(query_stack, (1, 0, 2)).reshape(QUERIES, IHEADS * IDIM)
    return (query_grad, key_grad)
```

```python
import functools
import math

import jax
import jax.numpy as jnp
from jax import lax
from jax.experimental import pallas as pl
from jax.experimental.pallas import tpu as pltpu
from jax.sharding import PartitionSpec as P

HEADS = 128
HEAD_DIM = 192
IDIM = 128
STRIDE = 8
NEG_FILL = -1e30
LOG2E = math.log2(math.e)
GROUP = 4
TILE = 16
SLOTS = 4
ORDER = (0, 2, 1, 3)
MESH = pl.DeviceIdType.MESH
F32 = jnp.float32
BF16 = jnp.bfloat16
NT = (((1,), (1,)), ((), ()))


def matmul_nt(a, b):
    return lax.dot_general(a, b, NT, preferred_element_type=F32)


def kernel(
    n_ctx, n_head, heads,
    q_hbm, k_hbm, iq_hbm, ik_ref, hwt_ref, qpos_ref, koff_ref,
    qgrad_ref, kgrad_ref,
    q_v, k_v, iq_v, probs, ikg, bias, lg_part, lg_recv, expo,
    stat_send, stat_recv, ist_send, ist_recv, w_send, w_recv, wi_ref,
    tg_part, tg_recv, pst, ps_send, ps_recv, kg_part, kg_recv, qg, hwb, hw_rows, hwt, iqo,
    sc0, sc1, sc2, sc3, tops,
    q_sem, k_sem, iq_sem, ag_s, ag_r, lg_s, lg_r, st_s, st_r, is_s, is_r,
    w_s, w_r, tg_s, tg_r, ps_s, ps_r, kg_s, kg_r,
):
    me = lax.axis_index("ctx")
    my_head = lax.axis_index("head")
    groups, row_tiles, _, group_width = q_v.shape
    rows = row_tiles * TILE
    pair_width = 2 * HEAD_DIM
    group = group_width // pair_width
    pairs = groups * group
    keys = k_v.shape[1]
    iheads = iq_v.shape[2] // IDIM
    own = rows // n_ctx
    own_tiles = own // TILE
    spread = row_tiles // SLOTS
    slot_rows = rows // SLOTS
    per_owner = max(1, 2 * pairs // n_ctx)
    split = n_ctx * per_owner // (2 * pairs)
    lanes_half = rows // 2
    part_rows = lanes_half // split
    score_scale = LOG2E / math.sqrt(HEAD_DIM)
    inv_scale = 1.0 / math.sqrt(IDIM)

    def peer_of(k, n, base):
        return lax.rem(base + k, n)

    def q_copy(p, slot):
        cols = pl.ds(pl.multiple_of(p * group_width, 128), group_width)
        return pltpu.make_async_copy(
            q_hbm.at[:, ORDER[slot], :, cols],
            q_v.at[p, pl.ds(slot * spread, spread)],
            q_sem.at[p, slot],
        )

    def k_copy(p):
        cols = pl.ds(pl.multiple_of(p * group_width, 128), group_width)
        return pltpu.make_async_copy(k_hbm.at[:, cols], k_v.at[p], k_sem.at[p])

    def iq_copy(slot):
        return pltpu.make_async_copy(
            iq_hbm.at[:, ORDER[slot]], iq_v.at[pl.ds(slot * spread, spread)], iq_sem.at[slot]
        )

    def iq_head(j, half=None):
        cols = pl.ds(pl.multiple_of(j * IDIM, 128), IDIM)
        if half is None:
            return iq_v[:, :, cols].reshape(rows, IDIM)
        first = half * (row_tiles // 2)
        return iq_v[first : first + row_tiles // 2, :, cols].reshape(lanes_half, IDIM)

    for slot in range(SLOTS):
        iq_copy(slot).start()

    @pl.loop(0, groups)
    def _(p):
        k_copy(p).start()
        for slot in range(SLOTS):
            q_copy(p, slot).start()

    barrier = pltpu.get_barrier_semaphore()
    for k in range(1, n_ctx):
        pl.semaphore_signal(
            barrier, inc=1, device_id={"ctx": peer_of(k, n_ctx, me)}, device_id_type=MESH
        )
    for k in range(1, n_head):
        pl.semaphore_signal(
            barrier, inc=1, device_id={"head": peer_of(k, n_head, my_head)}, device_id_type=MESH
        )

    ikg[me] = ik_ref[...].astype(F32)
    offset = jnp.broadcast_to(koff_ref[...].astype(F32), (128, keys)).T[:, 0:1].astype(jnp.int32)
    key_pos = STRIDE * (me * keys + lax.broadcasted_iota(jnp.int32, (keys, 1), 0)) + offset
    by_query = jnp.concatenate(
        [
            hwt_ref[...] * inv_scale,
            jnp.broadcast_to(qpos_ref[...].astype(F32), (128 - iheads, rows)),
        ],
        axis=0,
    ).T.reshape(spread, SLOTS, TILE, 128)
    by_query = jnp.concatenate(
        [by_query[:, ORDER[slot]].reshape(slot_rows, 128) for slot in range(SLOTS)], axis=0
    )
    hw_rows[...] = by_query
    by_lane = by_query.T
    hwt[...] = by_lane[:iheads]
    query_pos = by_lane[127:128].astype(jnp.int32)
    bias[...] = jnp.where(key_pos <= query_pos, 0.0, NEG_FILL)

    def own_tile(sub):
        tile = me * own_tiles + sub
        m = lax.rem(tile, SLOTS)
        return (lax.rem(m, 2) * 2 + lax.div(m, 2)) * spread + lax.div(tile, SLOTS)

    for sub in range(own_tiles):
        first = pl.multiple_of(own_tile(sub) * TILE, TILE)
        own_weights = hw_rows[pl.ds(first, TILE), :]
        for j in range(iheads):
            hwb[sub, j * TILE : (j + 1) * TILE, :] = jnp.broadcast_to(
                own_weights[:, j : j + 1], (TILE, 128)
            )
    lg_part[...] = jnp.zeros_like(lg_part)

    pl.semaphore_wait(barrier, n_ctx - 1 + n_head - 1)

    bits = [1 << b for b in reversed(range(n_ctx.bit_length() - 1))]
    stages = len(bits)
    turn = stages // 2
    orders = (bits, bits[turn:-1] + bits[:turn] + bits[-1:])

    def flip(index, bit):
        return index + bit * (1 - 2 * lax.rem(lax.div(index, bit), 2))

    def ag_shards(sub, stage, base):
        shards = [base]
        for bit in orders[sub][:stage]:
            shards = shards + [flip(s, bit) for s in shards]
        return shards

    sub_rows = keys // 2

    def ag_copy(shard, sub, stage):
        piece = ikg.at[shard, pl.ds(sub * sub_rows, sub_rows)]
        return pltpu.make_async_remote_copy(
            src_ref=piece, dst_ref=piece,
            send_sem=ag_s.at[stage, sub, shard], recv_sem=ag_r.at[sub, shard],
            device_id={"ctx": flip(me, orders[sub][stage])}, device_id_type=MESH,
        )

    def ag_start(sub, stage):
        for shard in ag_shards(sub, stage, me):
            ag_copy(shard, sub, stage).start()

    def ag_recv(sub, stage):
        for shard in ag_shards(sub, stage, flip(me, orders[sub][stage])):
            ag_copy(shard, sub, stage).wait_recv()

    def ag_sent(sub, stage):
        for shard in ag_shards(sub, stage, me):
            ag_copy(shard, sub, stage).wait_send()

    def ag_forward(event):
        sub, stage = event % 2, event // 2
        ag_recv(sub, stage)
        ag_start(sub, stage + 1)

    for sub in range(2):
        ag_start(sub, 0)

    for slot in range(SLOTS):
        iq_copy(slot).wait()

    @pl.loop(0, iheads, unroll=4)
    def _(j):
        act = matmul_nt(ik_ref[...], iq_head(j))
        lg_part[...] += hwt[pl.ds(j, 1), :] * jnp.maximum(act, 0.0)

    def head_copy(k, src, dst, send, recv):
        return pltpu.make_async_remote_copy(
            src_ref=src, dst_ref=dst, send_sem=send, recv_sem=recv,
            device_id={"head": peer_of(k, n_head, my_head)}, device_id_type=MESH,
        )

    def lg_copy(k, slot):
        return head_copy(k, lg_part, lg_recv.at[slot], lg_s.at[k], lg_r.at[slot])

    for k in range(1, n_head):
        lg_copy(k, my_head).start()

    def ctx_copy(k, src, dst, send, recv):
        return pltpu.make_async_remote_copy(
            src_ref=src, dst_ref=dst, send_sem=send, recv_sem=recv,
            device_id={"ctx": peer_of(k, n_ctx, me)}, device_id_type=MESH,
        )

    def stat_copy(h, k, peer, slot):
        return ctx_copy(
            k, stat_send.at[h, peer], stat_recv.at[h, slot], st_s.at[h, k], st_r.at[h, slot]
        )

    def ist_copy(k, slot):
        return ctx_copy(k, ist_send, ist_recv.at[slot], is_s.at[k], is_r.at[slot])

    def w_copy(h, k, peer, slot):
        return ctx_copy(k, w_send.at[h, peer], w_recv.at[h, slot], w_s.at[h, k], w_r.at[h, slot])

    def send_stats(h):
        @pl.loop(1, n_ctx)
        def _(k):
            stat_copy(h, k, peer_of(k, n_ctx, me), me).start()

        stat_recv[h, me] = stat_send[h, me]

    def send_weights(h):
        @pl.loop(1, n_ctx)
        def _(k):
            peer = peer_of(k, n_ctx, me)
            stat_copy(h, k, peer, peer).wait_recv()

        tops_all = stat_recv[h, :, :per_owner, :]
        masses = stat_recv[h, :, per_owner:, :]
        top = jnp.max(tops_all, axis=0, keepdims=True)
        shift = jnp.exp2(tops_all - top)
        total = jnp.sum(masses * shift, axis=0, keepdims=True)
        w_send[h] = shift * (1.0 / (HEADS * total))

        @pl.loop(1, n_ctx)
        def _(k):
            w_copy(h, k, peer_of(k, n_ctx, me), me).start()

        w_recv[h, me] = w_send[h, me]

    def recv_weights(h):
        @pl.loop(1, n_ctx)
        def _(k):
            peer = peer_of(k, n_ctx, me)
            w_copy(h, k, peer, peer).wait_recv()

    column = lax.broadcasted_iota(jnp.int32, (keys, 128), 1)
    rest = 256 - HEAD_DIM
    scores_refs = (sc0, sc1, sc2, sc3)

    def head_scores(h, p, b):
        a = b % 2
        place = lax.div(p, group)
        start = pl.multiple_of(lax.rem(p, group) * pair_width + a * 128, 128)
        near = k_v[place, :, pl.ds(start, 128)]
        far = k_v[place, :, pl.ds(pl.multiple_of(start + 128, 128), 128)]
        if a == 0:
            far = jnp.where(column < 128 - rest, far, jnp.zeros_like(far))
        else:
            near = jnp.where(column >= rest, near, jnp.zeros_like(near))
        first = h * (row_tiles // 2)
        query = q_v[place, first : first + row_tiles // 2, :, pl.ds(start, 256)]
        scores = matmul_nt(
            jnp.concatenate([near, far], axis=1), query.reshape(lanes_half, 256)
        )
        scores = scores * score_scale + bias[:, h * lanes_half : (h + 1) * lanes_half]
        scores_refs[b][...] = scores
        tops[b] = jnp.max(scores, axis=0, keepdims=True)

    def head_softmax(h, p, b):
        head = 2 * p + b % 2
        top = tops[b]
        expo_head = jnp.exp2(scores_refs[b][...] - top)
        mass = jnp.sum(expo_head, axis=0, keepdims=True)
        probs[head, :, h * lanes_half : (h + 1) * lanes_half] = expo_head.astype(BF16)
        owner = lax.div(head, per_owner) * split
        row = lax.rem(head, per_owner)
        for part in range(split):
            lanes = slice(part * part_rows, (part + 1) * part_rows)
            stat_send[h, owner + part, pl.ds(row, 1), :] = top[:, lanes]
            stat_send[h, owner + part, pl.ds(row + per_owner, 1), :] = mass[:, lanes]

    def wait_group(p):
        k_copy(p).wait()
        for slot in range(SLOTS):
            q_copy(p, slot).wait()

    def attention(h, events):
        if h == 0:
            wait_group(0)
        for b in range(4):
            head_scores(h, b // 2, b)

        @pl.loop(0, pairs // 4)
        def _(i):
            if h == 0:
                pl.when(i + 1 < groups)(lambda: wait_group(i + 1))
            for at, todo in events.items():
                pl.when(i == at)(todo)
            for u in range(2):
                p = 4 * i + 2 * u
                later = jnp.minimum(p + 2, pairs - 2)
                for b in range(4):
                    head_softmax(h, p + b // 2, b)
                    head_scores(h, later + b // 2, b)

        send_stats(h)

    steps = pairs // 4

    def forward_pair(stage):
        def run():
            for sub in range(2):
                ag_forward(2 * stage + sub)
        return run

    attention(0, {steps // 2: forward_pair(0)})
    attention(1, {steps // 4: forward_pair(1), (3 * steps) // 4: lambda: send_weights(0)})

    for k in range(1, n_head):
        slot = peer_of(k, n_head, my_head)
        lg_copy(k, slot).wait_recv()
    logits = lg_part[...]
    for k in range(1, n_head):
        logits = logits + lg_recv[peer_of(k, n_head, my_head)]
    logits = logits * (LOG2E) + bias[...]
    itop = jnp.max(logits, axis=0, keepdims=True)
    logits = jnp.exp2(logits - itop)
    expo[...] = logits
    ist_send[0:1, :] = itop
    ist_send[1:2, :] = jnp.sum(logits, axis=0, keepdims=True)

    @pl.loop(1, n_ctx)
    def _(k):
        ist_copy(k, me).start()

    ist_recv[me] = ist_send[...]

    for sub in range(own_tiles):
        tile = own_tile(sub)
        for j in range(iheads):
            iqo[sub, j * TILE : (j + 1) * TILE, :] = iq_v[tile, :, j * IDIM : (j + 1) * IDIM]
    qg[...] = jnp.zeros_like(qg)
    kg_part[...] = jnp.zeros_like(kg_part)

    def tg_copy(s, k, slot):
        return head_copy(
            k, tg_part.at[s], tg_recv.at[slot, s], tg_s.at[s, k], tg_r.at[s, slot]
        )

    def sum_heads(s):
        h, c = s // 2, s % 2
        part, start = c * slot_rows // part_rows, c * slot_rows % part_rows
        lanes = slice(s * slot_rows, (s + 1) * slot_rows)

        def add_owner(o, acc):
            weights = w_recv[h, o * split + part, :, start : start + slot_rows]
            for r in range(per_owner):
                terms = probs[o * per_owner + r, :, lanes]
                acc = acc + terms.astype(F32) * weights[r : r + 1]
            return acc

        tg_part[s] = lax.fori_loop(
            0, n_ctx // split, add_owner, jnp.zeros((keys, slot_rows), F32), unroll=2
        )
        for k in range(1, n_head):
            tg_copy(s, k, my_head).start()

    def ps_peer(s, i):
        return lax.div(i * SLOTS + ORDER[s], own_tiles)

    def ps_copy(s, i, peer, slot):
        sub = ORDER[s] % own_tiles
        return pltpu.make_async_remote_copy(
            src_ref=ps_send.at[s, i], dst_ref=ps_recv.at[sub, slot],
            send_sem=ps_s.at[s, i], recv_sem=ps_r.at[sub, slot],
            device_id={"ctx": peer}, device_id_type=MESH,
        )

    def each_peer(s, action):
        @pl.loop(0, spread)
        def _(k):
            i = lax.rem(lax.div(me * own_tiles, SLOTS) + k, spread)
            peer = ps_peer(s, i)

            @pl.when(peer != me)
            def _():
                action(ps_copy(s, i, peer, me))

    def send_step(s):
        for k in range(1, n_head):
            tg_copy(s, k, peer_of(k, n_head, my_head)).wait_recv()
        lanes = slice(s * slot_rows, (s + 1) * slot_rows)
        target = tg_part[s]
        for k in range(1, n_head):
            target = target + tg_recv[peer_of(k, n_head, my_head), s]
        step = expo[:, lanes] * wi_ref[:, lanes] - target
        pst[:, lanes] = step
        ps_send[s] = step.T.reshape(spread, TILE, keys)
        each_peer(s, lambda copy: copy.start())

    def key_grad_half(h):
        lanes = slice(h * lanes_half, (h + 1) * lanes_half)

        @pl.loop(0, iheads, unroll=4)
        def _(j):
            rows_j = iq_head(j, h)
            act = matmul_nt(ik_ref[...], rows_j)
            weighted = pst[:, lanes] * hwt[pl.ds(j, 1), lanes]
            terms = jnp.where(act > 0.0, weighted, 0.0).astype(BF16)
            kg_part[...] += jnp.dot(terms, rows_j, preferred_element_type=F32)

    recv_weights(0)
    sum_heads(0)
    sum_heads(1)
    send_weights(1)
    for stage in range(2, stages - 1):
        forward_pair(stage)()

    @pl.loop(1, n_ctx)
    def _(k):
        peer = peer_of(k, n_ctx, me)
        ist_copy(k, peer).wait_recv()

    itops = ist_recv[:, 0:1, :]
    imasses = ist_recv[:, 1:2, :]
    itop_all = jnp.max(itops, axis=0)
    itotal = jnp.sum(imasses * jnp.exp2(itops - itop_all[None]), axis=0)
    wi_ref[...] = jnp.exp2(ist_send[0:1, :] - itop_all) / itotal

    recv_weights(1)
    sum_heads(2)
    send_step(0)
    sum_heads(3)
    send_step(1)
    key_grad_half(0)
    send_step(2)
    send_step(3)
    for sub in range(own_tiles):
        tile = own_tile(sub)
        ps_recv[sub, me] = ps_send[lax.div(tile, spread), lax.rem(tile, spread)]
    key_grad_half(1)

    def kg_copy(k, slot):
        return head_copy(k, kg_part, kg_recv.at[slot], kg_s.at[k], kg_r.at[slot])

    for k in range(1, n_head):
        kg_copy(k, my_head).start()

    def add_source(sub, source):
        source_keys = ikg[source].astype(BF16)
        act = matmul_nt(iqo[sub], source_keys)
        terms = []
        for c in range(keys // 128):
            lanes = slice(c * 128, (c + 1) * 128)
            step = ps_recv[sub, source, :, lanes]
            weighted = hwb[sub].reshape(iheads, TILE, 128) * step[None]
            terms.append(
                jnp.where(
                    act[:, lanes] > 0.0, weighted.reshape(iheads * TILE, 128), 0.0
                ).astype(BF16)
            )
        qg[sub] += jnp.dot(
            jnp.concatenate(terms, axis=1), source_keys, preferred_element_type=F32
        )

    for sub in range(2):
        ag_recv(sub, stages - 1)

    for sub in range(own_tiles):
        add_source(sub, me)

        @pl.loop(1, n_ctx)
        def _(k):
            source = peer_of(k, n_ctx, me)
            ps_copy(ORDER.index(sub), 0, source, source).wait_recv()
            add_source(sub, source)

    for sub in range(own_tiles):
        for j in range(iheads):
            qgrad_ref[sub * TILE : (sub + 1) * TILE, j * IDIM : (j + 1) * IDIM] = qg[
                sub, j * TILE : (j + 1) * TILE, :
            ]

    key_grad = kg_part[...]
    for k in range(1, n_head):
        slot = peer_of(k, n_head, my_head)
        kg_copy(k, slot).wait_recv()
        key_grad = key_grad + kg_recv[slot]
    kgrad_ref[...] = key_grad

    for s in range(stages):
        for sub in range(2):
            ag_sent(sub, s)
    for k in range(1, n_head):
        lg_copy(k, my_head).wait_send()
        kg_copy(k, my_head).wait_send()
        for s in range(SLOTS):
            tg_copy(s, k, my_head).wait_send()

    @pl.loop(1, n_ctx)
    def _(k):
        peer = peer_of(k, n_ctx, me)
        ist_copy(k, me).wait_send()
        for h in range(2):
            stat_copy(h, k, peer, me).wait_send()
            w_copy(h, k, peer, me).wait_send()

    for s in range(SLOTS):
        each_peer(s, lambda copy: copy.wait_send())


def shards(n_ctx, n_head, queries, attn_keys, index_queries, index_keys, head_weights, query_pos, key_offset):
    rows = queries.shape[0]
    keys = attn_keys.shape[0]
    heads = attn_keys.shape[1] // HEAD_DIM
    iheads = index_queries.shape[1] // IDIM
    own_tiles = rows // n_ctx // TILE
    row_tiles = rows // TILE
    spread = row_tiles // SLOTS
    slot_rows = rows // SLOTS
    group = math.gcd(GROUP, heads // 2)
    groups = heads // 2 // group
    per_owner = max(1, heads // n_ctx)
    split = n_ctx * per_owner // heads
    stages = n_ctx.bit_length() - 1
    vmem = pltpu.VMEM
    dma = pltpu.SemaphoreType.DMA
    any_space = pl.BlockSpec(memory_space=pl.ANY)
    vmem_space = pl.BlockSpec(memory_space=pltpu.VMEM)
    return pl.pallas_call(
        functools.partial(kernel, n_ctx, n_head, heads),
        out_shape=(
            jax.ShapeDtypeStruct((rows // n_ctx, iheads * IDIM), F32),
            jax.ShapeDtypeStruct((keys, IDIM), F32),
        ),
        in_specs=[any_space] * 3 + [vmem_space] * 4,
        out_specs=(vmem_space, vmem_space),
        scratch_shapes=[
            vmem((groups, row_tiles, TILE, 2 * HEAD_DIM * group), BF16),
            vmem((groups, keys, 2 * HEAD_DIM * group), BF16),
            vmem((row_tiles, TILE, iheads * IDIM), BF16),
            vmem((heads, keys, rows), BF16),
            vmem((n_ctx, keys, IDIM), F32),
            vmem((keys, rows), F32),
            vmem((keys, rows), F32),
            vmem((n_head, keys, rows), F32),
            vmem((keys, rows), F32),
            vmem((2, n_ctx, 2 * per_owner, rows // 2 // split), F32),
            vmem((2, n_ctx, 2 * per_owner, rows // 2 // split), F32),
            vmem((2, rows), F32),
            vmem((n_ctx, 2, rows), F32),
            vmem((2, n_ctx, per_owner, rows // 2 // split), F32),
            vmem((2, n_ctx, per_owner, rows // 2 // split), F32),
            vmem((1, rows), F32),
            vmem((SLOTS, keys, slot_rows), F32),
            vmem((n_head, SLOTS, keys, slot_rows), F32),
            vmem((keys, rows), F32),
            vmem((SLOTS, spread, TILE, keys), F32),
            vmem((own_tiles, n_ctx, TILE, keys), F32),
            vmem((keys, IDIM), F32),
            vmem((n_head, keys, IDIM), F32),
            vmem((own_tiles, iheads * TILE, IDIM), F32),
            vmem((own_tiles, iheads * TILE, 128), F32),
            vmem((rows, 128), F32),
            vmem((iheads, rows), F32),
            vmem((own_tiles, iheads * TILE, IDIM), BF16),
            *[vmem((keys, rows // 2), F32)] * 4,
            vmem((4, 1, rows // 2), F32),
            dma((groups, SLOTS)),
            dma((groups,)),
            dma((SLOTS,)),
            dma((stages, 2, n_ctx)),
            dma((2, n_ctx)),
            dma((n_head,)),
            dma((n_head,)),
            dma((2, n_ctx)),
            dma((2, n_ctx)),
            dma((n_ctx,)),
            dma((n_ctx,)),
            dma((2, n_ctx)),
            dma((2, n_ctx)),
            dma((SLOTS, n_head)),
            dma((SLOTS, n_head)),
            dma((SLOTS, spread)),
            dma((own_tiles, n_ctx)),
            dma((n_head,)),
            dma((n_head,)),
        ],
        compiler_params=pltpu.CompilerParams(
            collective_id=0, has_side_effects=True, vmem_limit_bytes=64 * 1024 * 1024 - 65536
        ),
    )(
        queries.reshape(spread, SLOTS, TILE, queries.shape[1]),
        attn_keys,
        index_queries.reshape(spread, SLOTS, TILE, index_queries.shape[1]),
        index_keys,
        head_weights.T,
        query_pos.reshape(1, rows),
        key_offset.reshape(1, keys),
    )


def solution(mesh):
    in_specs = (
        P(None, "head"),
        P("ctx", "head"),
        P(None, "head"),
        P("ctx", None),
        P(None, "head"),
        P(),
        P("ctx"),
    )
    out_specs = (P("ctx", "head"), P("ctx", None))
    body = functools.partial(shards, mesh.shape["ctx"], mesh.shape["head"])
    return jax.shard_map(body, mesh=mesh, in_specs=in_specs, out_specs=out_specs, check_vma=False)
```

```python
import functools
import math

import jax
import jax.numpy as jnp
from jax import lax
from jax.experimental import pallas as pl
from jax.experimental.pallas import tpu as pltpu
from jax.sharding import PartitionSpec as P

HEADS = 128
HEAD_DIM = 192
IDIM = 128
STRIDE = 8
NEG_FILL = -1e30
LOG2E = math.log2(math.e)
GROUP = 4
BATCH = 8
SOURCES = 4
TILE = 16
SLOTS = 4
ORDER = (0, 2, 1, 3)
MESH = pl.DeviceIdType.MESH
F32 = jnp.float32
BF16 = jnp.bfloat16
NT = (((1,), (1,)), ((), ()))


def matmul_nt(a, b):
    return lax.dot_general(a, b, NT, preferred_element_type=F32)


def kernel(
    n_ctx, n_head, heads,
    q_hbm, k_hbm, iq_hbm, ik_ref, hwt_ref, qpos_ref, koff_ref,
    qgrad_ref, kgrad_ref,
    q_v, k_v, iq_v, probs, ikg, bias, lg_part, lg_recv, expo,
    stat_send, stat_recv, ist_send, ist_recv, w_send, w_recv, wi_ref,
    tg_part, tg_recv, pst, ps_send, ps_recv, kg_part, kg_recv, qg, hwb, hw_rows, hwt, iqo,
    sc0, sc1, sc2, sc3, tops, signs, acts,
    q_sem, k_sem, iq_sem, ag_s, ag_r, lg_s, lg_r, st_s, st_r, is_s, is_r,
    w_s, w_r, tg_s, tg_r, ps_s, ps_r, kg_s, kg_r,
):
    me = lax.axis_index("ctx")
    my_head = lax.axis_index("head")
    groups, row_tiles, _, group_width = q_v.shape
    rows = row_tiles * TILE
    pair_width = 2 * HEAD_DIM
    group = group_width // pair_width
    pairs = groups * group
    keys = k_v.shape[1]
    iheads = iq_v.shape[2] // IDIM
    own = rows // n_ctx
    own_tiles = own // TILE
    spread = row_tiles // SLOTS
    slot_rows = rows // SLOTS
    per_owner = max(1, 2 * pairs // n_ctx)
    split = n_ctx * per_owner // (2 * pairs)
    lanes_half = rows // 2
    part_rows = lanes_half // split
    score_scale = LOG2E / math.sqrt(HEAD_DIM)
    inv_scale = 1.0 / math.sqrt(IDIM)

    def peer_of(k, n, base):
        return lax.rem(base + k, n)

    def q_copy(p, slot):
        cols = pl.ds(pl.multiple_of(p * group_width, 128), group_width)
        return pltpu.make_async_copy(
            q_hbm.at[:, ORDER[slot], :, cols],
            q_v.at[p, pl.ds(slot * spread, spread)],
            q_sem.at[p, slot],
        )

    def k_copy(p):
        cols = pl.ds(pl.multiple_of(p * group_width, 128), group_width)
        return pltpu.make_async_copy(k_hbm.at[:, cols], k_v.at[p], k_sem.at[p])

    def iq_copy(slot):
        return pltpu.make_async_copy(
            iq_hbm.at[:, ORDER[slot]], iq_v.at[pl.ds(slot * spread, spread)], iq_sem.at[slot]
        )

    def iq_head(j, half):
        cols = pl.ds(pl.multiple_of(j * IDIM, 128), IDIM)
        first = half * (row_tiles // 2)
        return iq_v[first : first + row_tiles // 2, :, cols].reshape(lanes_half, IDIM)

    for slot in range(SLOTS):
        iq_copy(slot).start()

    @pl.loop(0, groups)
    def _(p):
        k_copy(p).start()
        for slot in range(SLOTS):
            q_copy(p, slot).start()

    barrier = pltpu.get_barrier_semaphore()
    for k in range(1, n_ctx):
        pl.semaphore_signal(
            barrier, inc=1, device_id={"ctx": peer_of(k, n_ctx, me)}, device_id_type=MESH
        )
    for k in range(1, n_head):
        pl.semaphore_signal(
            barrier, inc=1, device_id={"head": peer_of(k, n_head, my_head)}, device_id_type=MESH
        )

    ikg[me] = ik_ref[...].astype(F32)
    offset = jnp.broadcast_to(koff_ref[...].astype(F32), (128, keys)).T[:, 0:1].astype(jnp.int32)
    key_pos = STRIDE * (me * keys + lax.broadcasted_iota(jnp.int32, (keys, 1), 0)) + offset
    by_query = jnp.concatenate(
        [
            hwt_ref[...] * inv_scale,
            jnp.broadcast_to(qpos_ref[...].astype(F32), (128 - iheads, rows)),
        ],
        axis=0,
    ).T.reshape(spread, SLOTS, TILE, 128)
    by_query = jnp.concatenate(
        [by_query[:, ORDER[slot]].reshape(slot_rows, 128) for slot in range(SLOTS)], axis=0
    )
    hw_rows[...] = by_query
    by_lane = by_query.T
    hwt[...] = by_lane[:iheads]
    query_pos = by_lane[127:128].astype(jnp.int32)
    bias[...] = jnp.where(key_pos <= query_pos, 0.0, NEG_FILL)

    def own_tile(sub):
        tile = me * own_tiles + sub
        m = lax.rem(tile, SLOTS)
        return (lax.rem(m, 2) * 2 + lax.div(m, 2)) * spread + lax.div(tile, SLOTS)

    for sub in range(own_tiles):
        first = pl.multiple_of(own_tile(sub) * TILE, TILE)
        own_weights = hw_rows[pl.ds(first, TILE), :]
        for j in range(iheads):
            hwb[sub, j * TILE : (j + 1) * TILE, :] = jnp.broadcast_to(
                own_weights[:, j : j + 1], (TILE, 128)
            )
    lg_part[...] = jnp.zeros_like(lg_part)

    pl.semaphore_wait(barrier, n_ctx - 1 + n_head - 1)

    bits = [1 << b for b in reversed(range(n_ctx.bit_length() - 1))]
    stages = len(bits)
    turn = stages // 2
    orders = (bits, bits[turn:-1] + bits[:turn] + bits[-1:])

    def flip(index, bit):
        return index + bit * (1 - 2 * lax.rem(lax.div(index, bit), 2))

    def ag_shards(sub, stage, base):
        shards = [base]
        for bit in orders[sub][:stage]:
            shards = shards + [flip(s, bit) for s in shards]
        return shards

    sub_rows = keys // 2

    def ag_copy(shard, sub, stage):
        piece = ikg.at[shard, pl.ds(sub * sub_rows, sub_rows)]
        return pltpu.make_async_remote_copy(
            src_ref=piece, dst_ref=piece,
            send_sem=ag_s.at[stage, sub, shard], recv_sem=ag_r.at[sub, shard],
            device_id={"ctx": flip(me, orders[sub][stage])}, device_id_type=MESH,
        )

    def ag_start(sub, stage):
        for shard in ag_shards(sub, stage, me):
            ag_copy(shard, sub, stage).start()

    def ag_recv(sub, stage):
        for shard in ag_shards(sub, stage, flip(me, orders[sub][stage])):
            ag_copy(shard, sub, stage).wait_recv()

    def ag_sent(sub, stage):
        for shard in ag_shards(sub, stage, me):
            ag_copy(shard, sub, stage).wait_send()

    def ag_forward(sub, stage):
        ag_recv(sub, stage)
        ag_start(sub, stage + 1)

    for sub in range(2):
        ag_start(sub, 0)

    for slot in range(SLOTS):
        iq_copy(slot).wait()

    batch = math.gcd(BATCH, iheads)

    for h in range(2):
        half = slice(h * lanes_half, (h + 1) * lanes_half)

        @pl.loop(0, iheads // batch)
        def _(i):
            total = None
            for b in range(batch):
                j = i * batch + b
                act = matmul_nt(ik_ref[...], iq_head(j, h))
                signs[j, :, half] = act.astype(BF16)
                term = hwt[pl.ds(j, 1), half] * jnp.maximum(act, 0.0)
                total = term if total is None else total + term
            lg_part[:, half] += total

    def head_copy(k, src, dst, send, recv):
        return pltpu.make_async_remote_copy(
            src_ref=src, dst_ref=dst, send_sem=send, recv_sem=recv,
            device_id={"head": peer_of(k, n_head, my_head)}, device_id_type=MESH,
        )

    def lg_copy(k):
        return head_copy(k, lg_part, lg_recv.at[k - 1], lg_s.at[k], lg_r.at[k])

    for k in range(1, n_head):
        lg_copy(k).start()
    ag_forward(1, 0)

    def ctx_copy(k, src, dst, send, recv):
        return pltpu.make_async_remote_copy(
            src_ref=src, dst_ref=dst, send_sem=send, recv_sem=recv,
            device_id={"ctx": peer_of(k, n_ctx, me)}, device_id_type=MESH,
        )

    def stat_copy(h, k, peer, slot):
        return ctx_copy(
            k, stat_send.at[h, peer], stat_recv.at[h, slot], st_s.at[h, k], st_r.at[h, slot]
        )

    def ist_copy(k, slot):
        return ctx_copy(k, ist_send, ist_recv.at[slot], is_s.at[k], is_r.at[slot])

    def w_copy(h, k, peer, slot):
        return ctx_copy(k, w_send.at[h, peer], w_recv.at[h, slot], w_s.at[h, k], w_r.at[h, slot])

    def send_stats(h):
        @pl.loop(1, n_ctx)
        def _(k):
            stat_copy(h, k, peer_of(k, n_ctx, me), me).start()

        stat_recv[h, me] = stat_send[h, me]

    def send_weights(h):
        @pl.loop(1, n_ctx)
        def _(k):
            peer = peer_of(k, n_ctx, me)
            stat_copy(h, k, peer, peer).wait_recv()

        tops_all = stat_recv[h, :, :per_owner, :]
        masses = stat_recv[h, :, per_owner:, :]
        top = jnp.max(tops_all, axis=0, keepdims=True)
        shift = jnp.exp2(tops_all - top)
        total = jnp.sum(masses * shift, axis=0, keepdims=True)
        w_send[h] = shift * (1.0 / (HEADS * total))

        @pl.loop(1, n_ctx)
        def _(k):
            w_copy(h, k, peer_of(k, n_ctx, me), me).start()

        w_recv[h, me] = w_send[h, me]

    def recv_weights(h):
        @pl.loop(1, n_ctx)
        def _(k):
            peer = peer_of(k, n_ctx, me)
            w_copy(h, k, peer, peer).wait_recv()

    column = lax.broadcasted_iota(jnp.int32, (keys, 128), 1)
    rest = 256 - HEAD_DIM
    scores_refs = (sc0, sc1, sc2, sc3)

    def head_scores(h, p, b):
        a = b % 2
        place = lax.div(p, group)
        start = pl.multiple_of(lax.rem(p, group) * pair_width + a * 128, 128)
        near = k_v[place, :, pl.ds(start, 128)]
        far = k_v[place, :, pl.ds(pl.multiple_of(start + 128, 128), 128)]
        if a == 0:
            far = jnp.where(column < 128 - rest, far, jnp.zeros_like(far))
        else:
            near = jnp.where(column >= rest, near, jnp.zeros_like(near))
        first = h * (row_tiles // 2)
        query = q_v[place, first : first + row_tiles // 2, :, pl.ds(start, 256)]
        scores = matmul_nt(
            jnp.concatenate([near, far], axis=1), query.reshape(lanes_half, 256)
        )
        scores = scores * score_scale + bias[:, h * lanes_half : (h + 1) * lanes_half]
        scores_refs[b][...] = scores
        tops[b] = jnp.max(scores, axis=0, keepdims=True)

    def head_softmax(h, p, b):
        head = 2 * p + b % 2
        top = tops[b]
        expo_head = jnp.exp2(scores_refs[b][...] - top)
        mass = jnp.sum(expo_head, axis=0, keepdims=True)
        probs[head, :, h * lanes_half : (h + 1) * lanes_half] = expo_head.astype(BF16)
        owner = lax.div(head, per_owner) * split
        row = lax.rem(head, per_owner)
        for part in range(split):
            lanes = slice(part * part_rows, (part + 1) * part_rows)
            stat_send[h, owner + part, pl.ds(row, 1), :] = top[:, lanes]
            stat_send[h, owner + part, pl.ds(row + per_owner, 1), :] = mass[:, lanes]

    def wait_group(p):
        k_copy(p).wait()
        for slot in range(SLOTS):
            q_copy(p, slot).wait()

    def attention(h, events):
        if h == 0:
            wait_group(0)
        for b in range(4):
            head_scores(h, b // 2, b)

        @pl.loop(0, pairs // 4)
        def _(i):
            if h == 0:
                pl.when(i + 1 < groups)(lambda: wait_group(i + 1))
            for at, todo in events.items():
                pl.when(i == at)(todo)
            for u in range(2):
                p = 4 * i + 2 * u
                later = jnp.minimum(p + 2, pairs - 2)
                for b in range(4):
                    head_softmax(h, p + b // 2, b)
                    head_scores(h, later + b // 2, b)

        send_stats(h)

    steps = pairs // 4

    attention(0, {steps // 4: lambda: ag_forward(0, 0), steps - 1: lambda: ag_forward(0, 1)})
    attention(1, {(3 * steps) // 8: lambda: ag_forward(1, 1), (3 * steps) // 4: lambda: send_weights(0)})


    for k in range(1, n_head):
        lg_copy(k).wait_recv()
    logits = lg_part[...]
    for k in range(1, n_head):
        logits = logits + lg_recv[k - 1]
    logits = logits * (LOG2E) + bias[...]
    itop = jnp.max(logits, axis=0, keepdims=True)
    logits = jnp.exp2(logits - itop)
    expo[...] = logits
    ist_send[0:1, :] = itop
    ist_send[1:2, :] = jnp.sum(logits, axis=0, keepdims=True)

    @pl.loop(1, n_ctx)
    def _(k):
        ist_copy(k, me).start()

    ist_recv[me] = ist_send[...]

    for sub in range(own_tiles):
        tile = own_tile(sub)
        for j in range(iheads):
            iqo[sub, j * TILE : (j + 1) * TILE, :] = iq_v[tile, :, j * IDIM : (j + 1) * IDIM]
    qg[...] = jnp.zeros_like(qg)
    kg_part[...] = jnp.zeros_like(kg_part)

    def tg_copy(s, k):
        return head_copy(
            k, tg_part.at[s], tg_recv.at[k - 1, s], tg_s.at[s, k], tg_r.at[s, k]
        )

    def sum_heads(s):
        h, c = s // 2, s % 2
        part, start = c * slot_rows // part_rows, c * slot_rows % part_rows
        lanes = slice(s * slot_rows, (s + 1) * slot_rows)

        def add_owner(o, acc):
            weights = w_recv[h, o * split + part, :, start : start + slot_rows]
            for r in range(per_owner):
                terms = probs[o * per_owner + r, :, lanes]
                acc = acc + terms.astype(F32) * weights[r : r + 1]
            return acc

        tg_part[s] = lax.fori_loop(
            0, n_ctx // split, add_owner, jnp.zeros((keys, slot_rows), F32), unroll=2
        )
        for k in range(1, n_head):
            tg_copy(s, k).start()

    def ps_peer(s, i):
        return lax.div(i * SLOTS + ORDER[s], own_tiles)

    def ps_copy(s, i, peer, slot):
        sub = ORDER[s] % own_tiles
        return pltpu.make_async_remote_copy(
            src_ref=ps_send.at[s, i], dst_ref=ps_recv.at[sub, slot],
            send_sem=ps_s.at[s, i], recv_sem=ps_r.at[sub, slot],
            device_id={"ctx": peer}, device_id_type=MESH,
        )

    def each_peer(s, action):
        @pl.loop(0, spread)
        def _(k):
            i = lax.rem(lax.div(me * own_tiles, SLOTS) + k, spread)
            peer = ps_peer(s, i)

            @pl.when(peer != me)
            def _():
                action(ps_copy(s, i, peer, me))

    def send_step(s):
        for k in range(1, n_head):
            tg_copy(s, k).wait_recv()
        lanes = slice(s * slot_rows, (s + 1) * slot_rows)
        target = tg_part[s]
        for k in range(1, n_head):
            target = target + tg_recv[k - 1, s]
        step = expo[:, lanes] * wi_ref[:, lanes] - target
        pst[:, lanes] = step
        ps_send[s] = step.T.reshape(spread, TILE, keys)
        each_peer(s, lambda copy: copy.start())

    def key_grad_half(h):
        lanes = slice(h * lanes_half, (h + 1) * lanes_half)

        @pl.loop(0, iheads // batch)
        def _(i):
            terms, queries = [], []
            for b in range(batch):
                j = i * batch + b
                weighted = (pst[:, lanes] * hwt[pl.ds(j, 1), lanes]).astype(BF16)
                terms.append(jnp.where(signs[j, :, lanes] > 0, weighted, jnp.zeros_like(weighted)))
                queries.append(iq_head(j, h))
            kg_part[...] += jnp.dot(
                jnp.concatenate(terms, axis=1),
                jnp.concatenate(queries, axis=0),
                preferred_element_type=F32,
            )

    recv_weights(0)
    sum_heads(0)
    send_weights(1)
    sum_heads(1)
    for stage in range(2, stages - 1):
        for sub in range(2):
            ag_forward(sub, stage)

    @pl.loop(1, n_ctx)
    def _(k):
        peer = peer_of(k, n_ctx, me)
        ist_copy(k, peer).wait_recv()

    itops = ist_recv[:, 0:1, :]
    imasses = ist_recv[:, 1:2, :]
    itop_all = jnp.max(itops, axis=0)
    itotal = jnp.sum(imasses * jnp.exp2(itops - itop_all[None]), axis=0)
    wi_ref[...] = jnp.exp2(ist_send[0:1, :] - itop_all) / itotal

    recv_weights(1)
    sum_heads(2)
    send_step(0)
    sum_heads(3)
    send_step(1)
    key_grad_half(0)
    send_step(2)
    send_step(3)
    for sub in range(own_tiles):
        tile = own_tile(sub)
        ps_recv[sub, me] = ps_send[lax.div(tile, spread), lax.rem(tile, spread)]
    key_grad_half(1)

    def kg_copy(k):
        return head_copy(k, kg_part, kg_recv.at[k - 1], kg_s.at[k], kg_r.at[k])

    for k in range(1, n_head):
        kg_copy(k).start()

    def source_act(sub, source, b):
        acts[b] = matmul_nt(iqo[sub], ikg[source].astype(BF16))

    def source_terms(sub, source, b):
        terms = []
        for c in range(keys // 128):
            lanes = slice(c * 128, (c + 1) * 128)
            step = ps_recv[sub, source, :, lanes]
            weighted = (hwb[sub].reshape(iheads, TILE, 128) * step[None]).reshape(-1, 128)
            terms.append(jnp.where(acts[b, :, lanes] > 0.0, weighted, 0.0).astype(BF16))
        return terms

    for sub in range(2):
        ag_recv(sub, stages - 1)

    for sub in range(own_tiles):
        for b in range(SOURCES):
            source_act(sub, peer_of(b, n_ctx, me), b)

        @pl.loop(1, n_ctx)
        def _(k):
            source = peer_of(k, n_ctx, me)
            ps_copy(ORDER.index(sub), 0, source, source).wait_recv()

        @pl.loop(0, n_ctx // SOURCES)
        def _(i):
            terms, source_keys = [], []
            for b in range(SOURCES):
                source = peer_of(i * SOURCES + b, n_ctx, me)
                terms += source_terms(sub, source, b)
                source_keys.append(ikg[source].astype(BF16))
            qg[sub] += jnp.dot(
                jnp.concatenate(terms, axis=1),
                jnp.concatenate(source_keys, axis=0),
                preferred_element_type=F32,
            )
            later = jnp.minimum((i + 1) * SOURCES, n_ctx - SOURCES)
            for b in range(SOURCES):
                source_act(sub, peer_of(later + b, n_ctx, me), b)

    for sub in range(own_tiles):
        for j in range(iheads):
            qgrad_ref[sub * TILE : (sub + 1) * TILE, j * IDIM : (j + 1) * IDIM] = qg[
                sub, j * TILE : (j + 1) * TILE, :
            ]

    key_grad = kg_part[...]
    for k in range(1, n_head):
        kg_copy(k).wait_recv()
        key_grad = key_grad + kg_recv[k - 1]
    kgrad_ref[...] = key_grad

    for s in range(stages):
        for sub in range(2):
            ag_sent(sub, s)
    for k in range(1, n_head):
        lg_copy(k).wait_send()
        kg_copy(k).wait_send()
        for s in range(SLOTS):
            tg_copy(s, k).wait_send()

    @pl.loop(1, n_ctx)
    def _(k):
        peer = peer_of(k, n_ctx, me)
        ist_copy(k, me).wait_send()
        for h in range(2):
            stat_copy(h, k, peer, me).wait_send()
            w_copy(h, k, peer, me).wait_send()

    for s in range(SLOTS):
        each_peer(s, lambda copy: copy.wait_send())


def shards(n_ctx, n_head, queries, attn_keys, index_queries, index_keys, head_weights, query_pos, key_offset):
    rows = queries.shape[0]
    keys = attn_keys.shape[0]
    heads = attn_keys.shape[1] // HEAD_DIM
    iheads = index_queries.shape[1] // IDIM
    own_tiles = rows // n_ctx // TILE
    row_tiles = rows // TILE
    spread = row_tiles // SLOTS
    slot_rows = rows // SLOTS
    group = math.gcd(GROUP, heads // 2)
    groups = heads // 2 // group
    per_owner = max(1, heads // n_ctx)
    split = n_ctx * per_owner // heads
    stages = n_ctx.bit_length() - 1
    vmem = pltpu.VMEM
    dma = pltpu.SemaphoreType.DMA
    any_space = pl.BlockSpec(memory_space=pl.ANY)
    vmem_space = pl.BlockSpec(memory_space=pltpu.VMEM)
    return pl.pallas_call(
        functools.partial(kernel, n_ctx, n_head, heads),
        out_shape=(
            jax.ShapeDtypeStruct((rows // n_ctx, iheads * IDIM), F32),
            jax.ShapeDtypeStruct((keys, IDIM), F32),
        ),
        in_specs=[any_space] * 3 + [vmem_space] * 4,
        out_specs=(vmem_space, vmem_space),
        scratch_shapes=[
            vmem((groups, row_tiles, TILE, 2 * HEAD_DIM * group), BF16),
            vmem((groups, keys, 2 * HEAD_DIM * group), BF16),
            vmem((row_tiles, TILE, iheads * IDIM), BF16),
            vmem((heads, keys, rows), BF16),
            vmem((n_ctx, keys, IDIM), F32),
            vmem((keys, rows), F32),
            vmem((keys, rows), F32),
            vmem((n_head - 1, keys, rows), F32),
            vmem((keys, rows), F32),
            vmem((2, n_ctx, 2 * per_owner, rows // 2 // split), F32),
            vmem((2, n_ctx, 2 * per_owner, rows // 2 // split), F32),
            vmem((2, rows), F32),
            vmem((n_ctx, 2, rows), F32),
            vmem((2, n_ctx, per_owner, rows // 2 // split), F32),
            vmem((2, n_ctx, per_owner, rows // 2 // split), F32),
            vmem((1, rows), F32),
            vmem((SLOTS, keys, slot_rows), F32),
            vmem((n_head - 1, SLOTS, keys, slot_rows), F32),
            vmem((keys, rows), F32),
            vmem((SLOTS, spread, TILE, keys), F32),
            vmem((own_tiles, n_ctx, TILE, keys), F32),
            vmem((keys, IDIM), F32),
            vmem((n_head - 1, keys, IDIM), F32),
            vmem((own_tiles, iheads * TILE, IDIM), F32),
            vmem((own_tiles, iheads * TILE, 128), F32),
            vmem((rows, 128), F32),
            vmem((iheads, rows), F32),
            vmem((own_tiles, iheads * TILE, IDIM), BF16),
            *[vmem((keys, rows // 2), F32)] * 4,
            vmem((4, 1, rows // 2), F32),
            vmem((iheads, keys, rows), BF16),
            vmem((SOURCES, iheads * TILE, keys), F32),
            dma((groups, SLOTS)),
            dma((groups,)),
            dma((SLOTS,)),
            dma((stages, 2, n_ctx)),
            dma((2, n_ctx)),
            dma((n_head,)),
            dma((n_head,)),
            dma((2, n_ctx)),
            dma((2, n_ctx)),
            dma((n_ctx,)),
            dma((n_ctx,)),
            dma((2, n_ctx)),
            dma((2, n_ctx)),
            dma((SLOTS, n_head)),
            dma((SLOTS, n_head)),
            dma((SLOTS, spread)),
            dma((own_tiles, n_ctx)),
            dma((n_head,)),
            dma((n_head,)),
        ],
        compiler_params=pltpu.CompilerParams(
            collective_id=0, has_side_effects=True, vmem_limit_bytes=64 * 1024 * 1024 - 65536
        ),
    )(
        queries.reshape(spread, SLOTS, TILE, queries.shape[1]),
        attn_keys,
        index_queries.reshape(spread, SLOTS, TILE, index_queries.shape[1]),
        index_keys,
        head_weights.T,
        query_pos.reshape(1, rows),
        key_offset.reshape(1, keys),
    )


def solution(mesh):
    in_specs = (
        P(None, "head"),
        P("ctx", "head"),
        P(None, "head"),
        P("ctx", None),
        P(None, "head"),
        P(),
        P("ctx"),
    )
    out_specs = (P("ctx", "head"), P("ctx", None))
    body = functools.partial(shards, mesh.shape["ctx"], mesh.shape["head"])
    return jax.shard_map(body, mesh=mesh, in_specs=in_specs, out_specs=out_specs, check_vma=False)
```

```python
import functools
import math

import jax
import jax.numpy as jnp
from jax import lax
from jax.experimental import pallas as pl
from jax.experimental.pallas import tpu as pltpu
from jax.sharding import PartitionSpec as P

HEADS = 128
HEAD_DIM = 192
IDIM = 128
STRIDE = 8
NEG_FILL = -1e30
LOG2E = math.log2(math.e)
GROUP = 4
BATCH = 8
SOURCES = 4
TILE = 16
SLOTS = 4
ORDER = (0, 2, 1, 3)
MESH = pl.DeviceIdType.MESH
F32 = jnp.float32
BF16 = jnp.bfloat16
NT = (((1,), (1,)), ((), ()))


def matmul_nt(a, b):
    return lax.dot_general(a, b, NT, preferred_element_type=F32)


def kernel(
    n_ctx, n_head, heads,
    q_hbm, k_hbm, iq_hbm, ik_ref, hwt_ref, qpos_ref, koff_ref,
    qgrad_ref, kgrad_ref,
    q_v, k_v, iq_v, probs, ikg, bias, lg_part, lg_recv, expo,
    stat_send, stat_recv, top_own, ist_send, ist_recv, w_send, w_recv, wi_ref,
    tg_part, tg_recv, pst, ps_send, ps_recv, kg_part, kg_recv, qg, hwb, hw_rows, hwt, iqo,
    sc0, sc1, sc2, sc3, tops, signs, ikb,
    q_sem, k_sem, iq_sem, ag_s, ag_r, lg_s, lg_r, st_s, st_r, is_s, is_r,
    w_s, w_r, tg_s, tg_r, ps_s, ps_r, kg_s, kg_r,
):
    me = lax.axis_index("ctx")
    my_head = lax.axis_index("head")
    groups, row_tiles, _, group_width = q_v.shape
    rows = row_tiles * TILE
    pair_width = 2 * HEAD_DIM
    group = group_width // pair_width
    pairs = groups * group
    keys = k_v.shape[1]
    iheads = iq_v.shape[2] // IDIM
    own = rows // n_ctx
    own_tiles = own // TILE
    spread = row_tiles // SLOTS
    slot_rows = rows // SLOTS
    per_owner = max(1, 2 * pairs // n_ctx)
    split = n_ctx * per_owner // (2 * pairs)
    lanes_half = rows // 2
    part_rows = lanes_half // split
    score_scale = LOG2E / math.sqrt(HEAD_DIM)
    inv_scale = 1.0 / math.sqrt(IDIM)

    def peer_of(k, n, base):
        return lax.rem(base + k, n)

    def q_copy(p, slot):
        cols = pl.ds(pl.multiple_of(p * group_width, 128), group_width)
        return pltpu.make_async_copy(
            q_hbm.at[:, ORDER[slot], :, cols],
            q_v.at[p, pl.ds(slot * spread, spread)],
            q_sem.at[p, slot],
        )

    def k_copy(p):
        cols = pl.ds(pl.multiple_of(p * group_width, 128), group_width)
        return pltpu.make_async_copy(k_hbm.at[:, cols], k_v.at[p], k_sem.at[p])

    def iq_copy(slot):
        return pltpu.make_async_copy(
            iq_hbm.at[:, ORDER[slot]], iq_v.at[pl.ds(slot * spread, spread)], iq_sem.at[slot]
        )

    def iq_head(j, half):
        cols = pl.ds(pl.multiple_of(j * IDIM, 128), IDIM)
        first = half * (row_tiles // 2)
        return iq_v[first : first + row_tiles // 2, :, cols].reshape(lanes_half, IDIM)

    for slot in range(SLOTS):
        iq_copy(slot).start()

    @pl.loop(0, groups)
    def _(p):
        k_copy(p).start()
        for slot in range(SLOTS):
            q_copy(p, slot).start()

    barrier = pltpu.get_barrier_semaphore()
    for k in range(1, n_ctx):
        pl.semaphore_signal(
            barrier, inc=1, device_id={"ctx": peer_of(k, n_ctx, me)}, device_id_type=MESH
        )
    for k in range(1, n_head):
        pl.semaphore_signal(
            barrier, inc=1, device_id={"head": peer_of(k, n_head, my_head)}, device_id_type=MESH
        )

    ikg[me] = ik_ref[...].astype(F32)
    offset = jnp.broadcast_to(koff_ref[...].astype(F32), (128, keys)).T[:, 0:1].astype(jnp.int32)
    key_pos = STRIDE * (me * keys + lax.broadcasted_iota(jnp.int32, (keys, 1), 0)) + offset
    by_query = jnp.concatenate(
        [
            hwt_ref[...] * inv_scale,
            jnp.broadcast_to(qpos_ref[...].astype(F32), (128 - iheads, rows)),
        ],
        axis=0,
    ).T.reshape(spread, SLOTS, TILE, 128)
    by_query = jnp.concatenate(
        [by_query[:, ORDER[slot]].reshape(slot_rows, 128) for slot in range(SLOTS)], axis=0
    )
    hw_rows[...] = by_query
    by_lane = by_query.T
    hwt[...] = by_lane[:iheads]
    query_pos = by_lane[127:128].astype(jnp.int32)
    bias[...] = jnp.where(key_pos <= query_pos, 0.0, NEG_FILL)

    def own_tile(sub):
        tile = me * own_tiles + sub
        m = lax.rem(tile, SLOTS)
        return (lax.rem(m, 2) * 2 + lax.div(m, 2)) * spread + lax.div(tile, SLOTS)

    for sub in range(own_tiles):
        first = pl.multiple_of(own_tile(sub) * TILE, TILE)
        own_weights = hw_rows[pl.ds(first, TILE), :]
        for j in range(iheads):
            hwb[sub, j * TILE : (j + 1) * TILE, :] = jnp.broadcast_to(
                own_weights[:, j : j + 1], (TILE, 128)
            )
    lg_part[...] = jnp.zeros_like(lg_part)

    pl.semaphore_wait(barrier, n_ctx - 1 + n_head - 1)

    bits = [1 << b for b in reversed(range(n_ctx.bit_length() - 1))]
    stages = len(bits)
    turn = stages // 2
    orders = (bits, bits[turn:-1] + bits[:turn] + bits[-1:])

    def flip(index, bit):
        return index + bit * (1 - 2 * lax.rem(lax.div(index, bit), 2))

    def ag_shards(sub, stage, base):
        shards = [base]
        for bit in orders[sub][:stage]:
            shards = shards + [flip(s, bit) for s in shards]
        return shards

    sub_rows = keys // 2

    def ag_copy(shard, sub, stage):
        piece = ikg.at[shard, pl.ds(sub * sub_rows, sub_rows)]
        return pltpu.make_async_remote_copy(
            src_ref=piece, dst_ref=piece,
            send_sem=ag_s.at[stage, sub, shard], recv_sem=ag_r.at[sub, shard],
            device_id={"ctx": flip(me, orders[sub][stage])}, device_id_type=MESH,
        )

    def ag_start(sub, stage):
        for shard in ag_shards(sub, stage, me):
            ag_copy(shard, sub, stage).start()

    def ag_recv(sub, stage):
        for shard in ag_shards(sub, stage, flip(me, orders[sub][stage])):
            ag_copy(shard, sub, stage).wait_recv()

    def ag_sent(sub, stage):
        for shard in ag_shards(sub, stage, me):
            ag_copy(shard, sub, stage).wait_send()

    def ag_forward(sub, stage):
        ag_recv(sub, stage)
        ag_start(sub, stage + 1)

    for sub in range(2):
        ag_start(sub, 0)

    for slot in range(SLOTS):
        iq_copy(slot).wait()

    batch = math.gcd(BATCH, iheads)

    for h in range(2):
        half = slice(h * lanes_half, (h + 1) * lanes_half)

        @pl.loop(0, iheads // batch)
        def _(i):
            total = None
            for b in range(batch):
                j = i * batch + b
                act = matmul_nt(ik_ref[...], iq_head(j, h))
                signs[j, :, half] = act.astype(BF16)
                term = hwt[pl.ds(j, 1), half] * jnp.maximum(act, 0.0)
                total = term if total is None else total + term
            lg_part[:, half] += total

    def head_copy(k, src, dst, send, recv):
        return pltpu.make_async_remote_copy(
            src_ref=src, dst_ref=dst, send_sem=send, recv_sem=recv,
            device_id={"head": peer_of(k, n_head, my_head)}, device_id_type=MESH,
        )

    def lg_copy(k):
        return head_copy(k, lg_part, lg_recv.at[k - 1], lg_s.at[k], lg_r.at[k])

    for k in range(1, n_head):
        lg_copy(k).start()
    ag_forward(1, 0)

    def ctx_copy(k, src, dst, send, recv):
        return pltpu.make_async_remote_copy(
            src_ref=src, dst_ref=dst, send_sem=send, recv_sem=recv,
            device_id={"ctx": peer_of(k, n_ctx, me)}, device_id_type=MESH,
        )

    def stat_copy(h, k, peer, slot):
        return ctx_copy(
            k, stat_send.at[h, peer], stat_recv.at[h, slot], st_s.at[h, k], st_r.at[h, slot]
        )

    def ist_copy(k, slot):
        return ctx_copy(k, ist_send, ist_recv.at[slot], is_s.at[k], is_r.at[slot])

    def w_copy(h, k, slot):
        return ctx_copy(k, w_send.at[h], w_recv.at[h, slot], w_s.at[h, k], w_r.at[h, slot])

    def send_stats(h):
        stat_send[h] = top_own[h] + jnp.log2(stat_send[h])

        @pl.loop(1, n_ctx)
        def _(k):
            stat_copy(h, k, peer_of(k, n_ctx, me), me).start()

        stat_recv[h, me] = stat_send[h, me]

    def send_weights(h):
        @pl.loop(1, n_ctx)
        def _(k):
            peer = peer_of(k, n_ctx, me)
            stat_copy(h, k, peer, peer).wait_recv()

        levels = stat_recv[h]
        top = jnp.max(levels, axis=0)
        total = jnp.sum(jnp.exp2(levels - top[None]), axis=0)
        w_send[h] = top + jnp.log2(HEADS * total)

        @pl.loop(1, n_ctx)
        def _(k):
            w_copy(h, k, me).start()

        w_recv[h, me] = w_send[h]

    def recv_weights(h):
        @pl.loop(1, n_ctx)
        def _(k):
            w_copy(h, k, peer_of(k, n_ctx, me)).wait_recv()

        w_recv[h] = jnp.exp2(top_own[h] - w_recv[h])

    column = lax.broadcasted_iota(jnp.int32, (keys, 128), 1)
    rest = 256 - HEAD_DIM
    scores_refs = (sc0, sc1, sc2, sc3)

    def head_scores(h, p, b):
        a = b % 2
        place = lax.div(p, group)
        start = pl.multiple_of(lax.rem(p, group) * pair_width + a * 128, 128)
        near = k_v[place, :, pl.ds(start, 128)]
        far = k_v[place, :, pl.ds(pl.multiple_of(start + 128, 128), 128)]
        if a == 0:
            far = jnp.where(column < 128 - rest, far, jnp.zeros_like(far))
        else:
            near = jnp.where(column >= rest, near, jnp.zeros_like(near))
        first = h * (row_tiles // 2)
        query = q_v[place, first : first + row_tiles // 2, :, pl.ds(start, 256)]
        scores = matmul_nt(
            jnp.concatenate([near, far], axis=1), query.reshape(lanes_half, 256)
        )
        scores = scores * score_scale + bias[:, h * lanes_half : (h + 1) * lanes_half]
        scores_refs[b][...] = scores
        tops[b] = jnp.max(scores, axis=0, keepdims=True)

    def head_softmax(h, p, b):
        head = 2 * p + b % 2
        top = tops[b]
        expo_head = jnp.exp2(scores_refs[b][...] - top)
        mass = jnp.sum(expo_head, axis=0, keepdims=True)
        probs[head, :, h * lanes_half : (h + 1) * lanes_half] = expo_head.astype(BF16)
        owner = lax.div(head, per_owner) * split
        row = lax.rem(head, per_owner)
        for part in range(split):
            lanes = slice(part * part_rows, (part + 1) * part_rows)
            top_own[h, owner + part, pl.ds(row, 1), :] = top[:, lanes]
            stat_send[h, owner + part, pl.ds(row, 1), :] = mass[:, lanes]

    def wait_group(p):
        k_copy(p).wait()
        for slot in range(SLOTS):
            q_copy(p, slot).wait()

    def attention(h, events):
        if h == 0:
            wait_group(0)
        for b in range(4):
            head_scores(h, b // 2, b)

        @pl.loop(0, pairs // 4)
        def _(i):
            if h == 0:
                pl.when(i + 1 < groups)(lambda: wait_group(i + 1))
            for at, todo in events.items():
                pl.when(i == at)(todo)
            for u in range(2):
                p = 4 * i + 2 * u
                later = jnp.minimum(p + 2, pairs - 2)
                for b in range(4):
                    head_softmax(h, p + b // 2, b)
                    head_scores(h, later + b // 2, b)

        send_stats(h)

    steps = pairs // 4

    attention(0, {steps // 4: lambda: ag_forward(0, 0), steps - 1: lambda: ag_forward(0, 1)})
    attention(1, {(3 * steps) // 8: lambda: ag_forward(1, 1), (3 * steps) // 4: lambda: send_weights(0)})


    for k in range(1, n_head):
        lg_copy(k).wait_recv()
    logits = lg_part[...]
    for k in range(1, n_head):
        logits = logits + lg_recv[k - 1]
    logits = logits * (LOG2E) + bias[...]
    itop = jnp.max(logits, axis=0, keepdims=True)
    logits = jnp.exp2(logits - itop)
    expo[...] = logits
    ist_send[0:1, :] = itop
    ist_send[1:2, :] = jnp.sum(logits, axis=0, keepdims=True)

    @pl.loop(1, n_ctx)
    def _(k):
        ist_copy(k, me).start()

    ist_recv[me] = ist_send[...]

    for sub in range(own_tiles):
        tile = own_tile(sub)
        for j in range(iheads):
            iqo[sub, j * TILE : (j + 1) * TILE, :] = iq_v[tile, :, j * IDIM : (j + 1) * IDIM]
    qg[...] = jnp.zeros_like(qg)
    kg_part[...] = jnp.zeros_like(kg_part)

    def tg_copy(s, k):
        return head_copy(
            k, tg_part.at[s], tg_recv.at[k - 1, s], tg_s.at[s, k], tg_r.at[s, k]
        )

    def sum_heads(s):
        h, c = s // 2, s % 2
        part, start = c * slot_rows // part_rows, c * slot_rows % part_rows
        lanes = slice(s * slot_rows, (s + 1) * slot_rows)

        def add_owner(o, acc):
            weights = w_recv[h, o * split + part, :, start : start + slot_rows]
            for r in range(per_owner):
                terms = probs[o * per_owner + r, :, lanes]
                acc = acc + terms.astype(F32) * weights[r : r + 1]
            return acc

        tg_part[s] = lax.fori_loop(
            0, n_ctx // split, add_owner, jnp.zeros((keys, slot_rows), F32), unroll=2
        )
        for k in range(1, n_head):
            tg_copy(s, k).start()

    def ps_peer(s, i):
        return lax.div(i * SLOTS + ORDER[s], own_tiles)

    def ps_copy(s, i, peer, slot):
        sub = ORDER[s] % own_tiles
        return pltpu.make_async_remote_copy(
            src_ref=ps_send.at[s, i], dst_ref=ps_recv.at[sub, slot],
            send_sem=ps_s.at[s, i], recv_sem=ps_r.at[sub, slot],
            device_id={"ctx": peer}, device_id_type=MESH,
        )

    def each_peer(s, action):
        @pl.loop(0, spread)
        def _(k):
            i = lax.rem(lax.div(me * own_tiles, SLOTS) + k, spread)
            peer = ps_peer(s, i)

            @pl.when(peer != me)
            def _():
                action(ps_copy(s, i, peer, me))

    def send_step(s):
        for k in range(1, n_head):
            tg_copy(s, k).wait_recv()
        lanes = slice(s * slot_rows, (s + 1) * slot_rows)
        target = tg_part[s]
        for k in range(1, n_head):
            target = target + tg_recv[k - 1, s]
        step = expo[:, lanes] * wi_ref[:, lanes] - target
        pst[:, lanes] = step
        ps_send[s] = step.T.reshape(spread, TILE, keys)
        each_peer(s, lambda copy: copy.start())

    tall = row_tiles // iheads
    wide = group_width // keys

    def sign_place(n, first, width):
        rem = lax.rem(n, tall * wide)
        cols = pl.ds(pl.multiple_of(lax.div(rem, tall) * keys + first, 128), width)
        return (
            lax.div(n, tall * wide),
            pl.ds(lax.rem(rem, tall) * iheads, iheads),
            slice(None),
            cols,
        )

    def query_signs(sub):
        @pl.loop(0, n_ctx // SOURCES)
        def _(g):
            for b in range(SOURCES):
                i = g * SOURCES + b
                source_keys = ikg[peer_of(i, n_ctx, me)].astype(BF16)
                if sub == 0:
                    ikb[i] = source_keys
                act = matmul_nt(iqo[sub], source_keys).astype(BF16)
                q_v[sign_place(sub * n_ctx + i, 0, keys)] = act.reshape(iheads, TILE, keys)

    def key_grad_half(h):
        lanes = slice(h * lanes_half, (h + 1) * lanes_half)

        @pl.loop(0, iheads // batch)
        def _(i):
            terms, queries = [], []
            for b in range(batch):
                j = i * batch + b
                weighted = (pst[:, lanes] * hwt[pl.ds(j, 1), lanes]).astype(BF16)
                terms.append(jnp.where(signs[j, :, lanes] > 0, weighted, jnp.zeros_like(weighted)))
                queries.append(iq_head(j, h))
            kg_part[...] += jnp.dot(
                jnp.concatenate(terms, axis=1),
                jnp.concatenate(queries, axis=0),
                preferred_element_type=F32,
            )

    recv_weights(0)
    sum_heads(0)
    send_weights(1)
    sum_heads(1)
    for stage in range(2, stages - 1):
        for sub in range(2):
            ag_forward(sub, stage)

    @pl.loop(1, n_ctx)
    def _(k):
        peer = peer_of(k, n_ctx, me)
        ist_copy(k, peer).wait_recv()

    itops = ist_recv[:, 0:1, :]
    imasses = ist_recv[:, 1:2, :]
    itop_all = jnp.max(itops, axis=0)
    itotal = jnp.sum(imasses * jnp.exp2(itops - itop_all[None]), axis=0)
    wi_ref[...] = jnp.exp2(ist_send[0:1, :] - itop_all) / itotal

    for sub in range(2):
        ag_recv(sub, stages - 1)
    query_signs(0)
    recv_weights(1)
    sum_heads(2)
    send_step(0)
    sum_heads(3)
    send_step(1)
    key_grad_half(0)
    send_step(2)
    send_step(3)
    for sub in range(own_tiles):
        tile = own_tile(sub)
        ps_recv[sub, me] = ps_send[lax.div(tile, spread), lax.rem(tile, spread)]
    key_grad_half(1)

    def kg_copy(k):
        return head_copy(k, kg_part, kg_recv.at[k - 1], kg_s.at[k], kg_r.at[k])

    for k in range(1, n_head):
        kg_copy(k).start()

    for sub in range(1, own_tiles):
        query_signs(sub)

    def source_terms(sub, i, source):
        terms = []
        for c in range(keys // 128):
            lanes = slice(c * 128, (c + 1) * 128)
            step = ps_recv[sub, source, :, lanes]
            weighted = (hwb[sub].reshape(iheads, TILE, 128) * step[None]).astype(BF16)
            act = q_v[sign_place(sub * n_ctx + i, c * 128, 128)]
            terms.append(
                jnp.where(act > 0, weighted, jnp.zeros_like(weighted)).reshape(-1, 128)
            )
        return terms

    for sub in range(own_tiles):
        @pl.loop(1, n_ctx)
        def _(k):
            source = peer_of(k, n_ctx, me)
            ps_copy(ORDER.index(sub), 0, source, source).wait_recv()

        @pl.loop(0, n_ctx // SOURCES)
        def _(g):
            terms, source_keys = [], []
            for b in range(SOURCES):
                i = g * SOURCES + b
                terms += source_terms(sub, i, peer_of(i, n_ctx, me))
                source_keys.append(ikb[i])
            qg[sub] += jnp.dot(
                jnp.concatenate(terms, axis=1),
                jnp.concatenate(source_keys, axis=0),
                preferred_element_type=F32,
            )

    for sub in range(own_tiles):
        for j in range(iheads):
            qgrad_ref[sub * TILE : (sub + 1) * TILE, j * IDIM : (j + 1) * IDIM] = qg[
                sub, j * TILE : (j + 1) * TILE, :
            ]

    key_grad = kg_part[...]
    for k in range(1, n_head):
        kg_copy(k).wait_recv()
        key_grad = key_grad + kg_recv[k - 1]
    kgrad_ref[...] = key_grad

    for s in range(stages):
        for sub in range(2):
            ag_sent(sub, s)
    for k in range(1, n_head):
        lg_copy(k).wait_send()
        kg_copy(k).wait_send()
        for s in range(SLOTS):
            tg_copy(s, k).wait_send()

    @pl.loop(1, n_ctx)
    def _(k):
        peer = peer_of(k, n_ctx, me)
        ist_copy(k, me).wait_send()
        for h in range(2):
            stat_copy(h, k, peer, me).wait_send()
            w_copy(h, k, me).wait_send()

    for s in range(SLOTS):
        each_peer(s, lambda copy: copy.wait_send())


def hand_on(query_ref, key_ref, query_out, key_out):
    query_out[...] = query_ref[...]
    key_out[...] = key_ref[...]


def shards(n_ctx, n_head, queries, attn_keys, index_queries, index_keys, head_weights, query_pos, key_offset):
    rows = queries.shape[0]
    keys = attn_keys.shape[0]
    heads = attn_keys.shape[1] // HEAD_DIM
    iheads = index_queries.shape[1] // IDIM
    own_tiles = rows // n_ctx // TILE
    row_tiles = rows // TILE
    spread = row_tiles // SLOTS
    slot_rows = rows // SLOTS
    group = math.gcd(GROUP, heads // 2)
    groups = heads // 2 // group
    per_owner = max(1, heads // n_ctx)
    split = n_ctx * per_owner // heads
    stages = n_ctx.bit_length() - 1
    vmem = pltpu.VMEM
    dma = pltpu.SemaphoreType.DMA
    any_space = pl.BlockSpec(memory_space=pl.ANY)
    vmem_space = pl.BlockSpec(memory_space=pltpu.VMEM)
    query_grad, key_grad = pl.pallas_call(
        functools.partial(kernel, n_ctx, n_head, heads),
        out_shape=(
            jax.ShapeDtypeStruct((rows // n_ctx, iheads * IDIM), F32),
            jax.ShapeDtypeStruct((keys, IDIM), F32),
        ),
        in_specs=[any_space] * 3 + [vmem_space] * 4,
        out_specs=(vmem_space, vmem_space),
        scratch_shapes=[
            vmem((groups, row_tiles, TILE, 2 * HEAD_DIM * group), BF16),
            vmem((groups, keys, 2 * HEAD_DIM * group), BF16),
            vmem((row_tiles, TILE, iheads * IDIM), BF16),
            vmem((heads, keys, rows), BF16),
            vmem((n_ctx, keys, IDIM), F32),
            vmem((keys, rows), F32),
            vmem((keys, rows), F32),
            vmem((n_head - 1, keys, rows), F32),
            vmem((keys, rows), F32),
            vmem((2, n_ctx, per_owner, rows // 2 // split), F32),
            vmem((2, n_ctx, per_owner, rows // 2 // split), F32),
            vmem((2, n_ctx, per_owner, rows // 2 // split), F32),
            vmem((2, rows), F32),
            vmem((n_ctx, 2, rows), F32),
            vmem((2, per_owner, rows // 2 // split), F32),
            vmem((2, n_ctx, per_owner, rows // 2 // split), F32),
            vmem((1, rows), F32),
            vmem((SLOTS, keys, slot_rows), F32),
            vmem((n_head - 1, SLOTS, keys, slot_rows), F32),
            vmem((keys, rows), F32),
            vmem((SLOTS, spread, TILE, keys), F32),
            vmem((own_tiles, n_ctx, TILE, keys), F32),
            vmem((keys, IDIM), F32),
            vmem((n_head - 1, keys, IDIM), F32),
            vmem((own_tiles, iheads * TILE, IDIM), F32),
            vmem((own_tiles, iheads * TILE, 128), F32),
            vmem((rows, 128), F32),
            vmem((iheads, rows), F32),
            vmem((own_tiles, iheads * TILE, IDIM), BF16),
            *[vmem((keys, rows // 2), F32)] * 4,
            vmem((4, 1, rows // 2), F32),
            vmem((iheads, keys, rows), BF16),
            vmem((n_ctx, keys, IDIM), BF16),
            dma((groups, SLOTS)),
            dma((groups,)),
            dma((SLOTS,)),
            dma((stages, 2, n_ctx)),
            dma((2, n_ctx)),
            dma((n_head,)),
            dma((n_head,)),
            dma((2, n_ctx)),
            dma((2, n_ctx)),
            dma((n_ctx,)),
            dma((n_ctx,)),
            dma((2, n_ctx)),
            dma((2, n_ctx)),
            dma((SLOTS, n_head)),
            dma((SLOTS, n_head)),
            dma((SLOTS, spread)),
            dma((own_tiles, n_ctx)),
            dma((n_head,)),
            dma((n_head,)),
        ],
        compiler_params=pltpu.CompilerParams(
            collective_id=0, has_side_effects=True, vmem_limit_bytes=64 * 1024 * 1024 - 65536
        ),
    )(
        queries.reshape(spread, SLOTS, TILE, queries.shape[1]),
        attn_keys,
        index_queries.reshape(spread, SLOTS, TILE, index_queries.shape[1]),
        index_keys,
        head_weights.T,
        query_pos.reshape(1, rows),
        key_offset.reshape(1, keys),
    )
    return pl.pallas_call(
        hand_on,
        out_shape=(
            jax.ShapeDtypeStruct(query_grad.shape, F32),
            jax.ShapeDtypeStruct(key_grad.shape, F32),
        ),
        in_specs=[vmem_space] * 2,
        out_specs=(vmem_space, vmem_space),
    )(query_grad, key_grad)


def solution(mesh):
    in_specs = (
        P(None, "head"),
        P("ctx", "head"),
        P(None, "head"),
        P("ctx", None),
        P(None, "head"),
        P(),
        P("ctx"),
    )
    out_specs = (P("ctx", "head"), P("ctx", None))
    body = functools.partial(shards, mesh.shape["ctx"], mesh.shape["head"])
    return jax.shard_map(body, mesh=mesh, in_specs=in_specs, out_specs=out_specs, check_vma=False)
```

```python
import functools
import math

import jax
import jax.numpy as jnp
from jax import lax
from jax.experimental import pallas as pl
from jax.experimental.pallas import tpu as pltpu
from jax.sharding import PartitionSpec as P

HEADS = 128
HEAD_DIM = 192
IDIM = 128
STRIDE = 8
NEG_FILL = -1e30
LOG2E = math.log2(math.e)
GROUP = 4
BATCH = 8
SOURCES = 4
TILE = 16
SLOTS = 4
ORDER = (0, 2, 1, 3)
MESH = pl.DeviceIdType.MESH
F32 = jnp.float32
BF16 = jnp.bfloat16
NT = (((1,), (1,)), ((), ()))


def matmul_nt(a, b):
    return lax.dot_general(a, b, NT, preferred_element_type=F32)


def kernel(
    n_ctx, n_head, heads,
    q_hbm, k_hbm, iq_hbm, ik_ref, hwt_ref, qpos_ref, koff_ref,
    qgrad_ref, kgrad_ref,
    q_v, k_v, iq_v, probs, ikg, bias, lg_part, lg_recv, expo,
    stat_send, stat_recv, top_own, ist_send, ist_recv, w_send, w_recv, wi_ref,
    tg_part, tg_recv, pst, ps_send, ps_recv, kg_part, kg_recv, qg, hwb, hw_rows, hwt, iqo,
    sc0, sc1, sc2, sc3, tops, signs, ikb,
    q_sem, k_sem, iq_sem, ag_s, ag_r, lg_s, lg_r, st_s, st_r, is_s, is_r,
    w_s, w_r, tg_s, tg_r, ps_s, ps_r, kg_s, kg_r,
):
    me = lax.axis_index("ctx")
    my_head = lax.axis_index("head")
    groups, row_tiles, _, group_width = q_v.shape
    rows = row_tiles * TILE
    pair_width = 2 * HEAD_DIM
    group = group_width // pair_width
    pairs = groups * group
    keys = k_v.shape[1]
    iheads = iq_v.shape[2] // IDIM
    own = rows // n_ctx
    own_tiles = own // TILE
    spread = row_tiles // SLOTS
    slot_rows = rows // SLOTS
    per_owner = max(1, 2 * pairs // n_ctx)
    split = n_ctx * per_owner // (2 * pairs)
    lanes_half = rows // 2
    part_rows = lanes_half // split
    score_scale = LOG2E / math.sqrt(HEAD_DIM)
    inv_scale = 1.0 / math.sqrt(IDIM)

    def peer_of(k, n, base):
        return lax.rem(base + k, n)

    def q_copy(p, slot):
        cols = pl.ds(pl.multiple_of(p * group_width, 128), group_width)
        return pltpu.make_async_copy(
            q_hbm.at[:, ORDER[slot], :, cols],
            q_v.at[p, pl.ds(slot * spread, spread)],
            q_sem.at[p, slot],
        )

    def k_copy(p):
        cols = pl.ds(pl.multiple_of(p * group_width, 128), group_width)
        return pltpu.make_async_copy(k_hbm.at[:, cols], k_v.at[p], k_sem.at[p])

    def iq_copy(slot):
        return pltpu.make_async_copy(
            iq_hbm.at[:, ORDER[slot]], iq_v.at[pl.ds(slot * spread, spread)], iq_sem.at[slot]
        )

    def iq_head(j, half):
        cols = pl.ds(pl.multiple_of(j * IDIM, 128), IDIM)
        first = half * (row_tiles // 2)
        return iq_v[first : first + row_tiles // 2, :, cols].reshape(lanes_half, IDIM)

    for slot in range(SLOTS):
        iq_copy(slot).start()

    @pl.loop(0, groups)
    def _(p):
        k_copy(p).start()
        for slot in range(SLOTS):
            q_copy(p, slot).start()

    barrier = pltpu.get_barrier_semaphore()
    for k in range(1, n_ctx):
        pl.semaphore_signal(
            barrier, inc=1, device_id={"ctx": peer_of(k, n_ctx, me)}, device_id_type=MESH
        )
    for k in range(1, n_head):
        pl.semaphore_signal(
            barrier, inc=1, device_id={"head": peer_of(k, n_head, my_head)}, device_id_type=MESH
        )

    ikg[me] = ik_ref[...].astype(F32)
    offset = jnp.broadcast_to(koff_ref[...].astype(F32), (128, keys)).T[:, 0:1].astype(jnp.int32)
    key_pos = STRIDE * (me * keys + lax.broadcasted_iota(jnp.int32, (keys, 1), 0)) + offset
    by_query = jnp.concatenate(
        [
            hwt_ref[...] * inv_scale,
            jnp.broadcast_to(qpos_ref[...].astype(F32), (128 - iheads, rows)),
        ],
        axis=0,
    ).T.reshape(spread, SLOTS, TILE, 128)
    by_query = jnp.concatenate(
        [by_query[:, ORDER[slot]].reshape(slot_rows, 128) for slot in range(SLOTS)], axis=0
    )
    hw_rows[...] = by_query
    by_lane = by_query.T
    hwt[...] = by_lane[:iheads]
    query_pos = by_lane[127:128].astype(jnp.int32)
    bias[...] = jnp.where(key_pos <= query_pos, 0.0, NEG_FILL)

    def own_tile(sub):
        tile = me * own_tiles + sub
        m = lax.rem(tile, SLOTS)
        return (lax.rem(m, 2) * 2 + lax.div(m, 2)) * spread + lax.div(tile, SLOTS)

    pl.semaphore_wait(barrier, n_ctx - 1 + n_head - 1)

    bits = [1 << b for b in reversed(range(n_ctx.bit_length() - 1))]
    stages = len(bits)
    turn = stages // 2
    orders = (bits, bits[turn:-1] + bits[:turn] + bits[-1:])

    def flip(index, bit):
        return index + bit * (1 - 2 * lax.rem(lax.div(index, bit), 2))

    def ag_shards(sub, stage, base):
        shards = [base]
        for bit in orders[sub][:stage]:
            shards = shards + [flip(s, bit) for s in shards]
        return shards

    sub_rows = keys // 2

    def ag_copy(shard, sub, stage):
        piece = ikg.at[shard, pl.ds(sub * sub_rows, sub_rows)]
        return pltpu.make_async_remote_copy(
            src_ref=piece, dst_ref=piece,
            send_sem=ag_s.at[stage, sub, shard], recv_sem=ag_r.at[sub, shard],
            device_id={"ctx": flip(me, orders[sub][stage])}, device_id_type=MESH,
        )

    def ag_start(sub, stage):
        for shard in ag_shards(sub, stage, me):
            ag_copy(shard, sub, stage).start()

    def ag_recv(sub, stage):
        for shard in ag_shards(sub, stage, flip(me, orders[sub][stage])):
            ag_copy(shard, sub, stage).wait_recv()

    def ag_sent(sub, stage):
        for shard in ag_shards(sub, stage, me):
            ag_copy(shard, sub, stage).wait_send()

    def ag_forward(sub, stage):
        ag_recv(sub, stage)
        ag_start(sub, stage + 1)

    for sub in range(2):
        ag_start(sub, 0)

    for slot in range(SLOTS):
        iq_copy(slot).wait()

    batch = math.gcd(BATCH, iheads)

    def index_forward(h):
        half = slice(h * lanes_half, (h + 1) * lanes_half)
        lg_part[h] = jnp.zeros_like(lg_part[h])

        @pl.loop(0, iheads // batch)
        def _(i):
            total = None
            for b in range(batch):
                j = i * batch + b
                act = matmul_nt(ik_ref[...], iq_head(j, h))
                signs[j, :, half] = act.astype(BF16)
                term = hwt[pl.ds(j, 1), half] * jnp.maximum(act, 0.0)
                total = term if total is None else total + term
            lg_part[h] += total

        for k in range(1, n_head):
            lg_copy(h, k).start()

    def head_copy(k, src, dst, send, recv):
        return pltpu.make_async_remote_copy(
            src_ref=src, dst_ref=dst, send_sem=send, recv_sem=recv,
            device_id={"head": peer_of(k, n_head, my_head)}, device_id_type=MESH,
        )

    def lg_copy(h, k):
        return head_copy(k, lg_part.at[h], lg_recv.at[k - 1, h], lg_s.at[h, k], lg_r.at[h, k])

    index_forward(0)

    def ctx_copy(k, src, dst, send, recv):
        return pltpu.make_async_remote_copy(
            src_ref=src, dst_ref=dst, send_sem=send, recv_sem=recv,
            device_id={"ctx": peer_of(k, n_ctx, me)}, device_id_type=MESH,
        )

    def stat_copy(h, k, peer, slot):
        return ctx_copy(
            k, stat_send.at[h, peer], stat_recv.at[h, slot], st_s.at[h, k], st_r.at[h, slot]
        )

    def ist_copy(h, k, slot):
        return ctx_copy(k, ist_send.at[h], ist_recv.at[h, slot], is_s.at[h, k], is_r.at[h, slot])

    def w_copy(h, k, slot):
        return ctx_copy(k, w_send.at[h], w_recv.at[h, slot], w_s.at[h, k], w_r.at[h, slot])

    def send_stats(h):
        stat_send[h] = top_own[h] + jnp.log2(stat_send[h])

        @pl.loop(1, n_ctx)
        def _(k):
            stat_copy(h, k, peer_of(k, n_ctx, me), me).start()

        stat_recv[h, me] = stat_send[h, me]

    def send_weights(h):
        @pl.loop(1, n_ctx)
        def _(k):
            peer = peer_of(k, n_ctx, me)
            stat_copy(h, k, peer, peer).wait_recv()

        levels = stat_recv[h]
        top = jnp.max(levels, axis=0)
        total = jnp.sum(jnp.exp2(levels - top[None]), axis=0)
        w_send[h] = top + jnp.log2(HEADS * total)

        @pl.loop(1, n_ctx)
        def _(k):
            w_copy(h, k, me).start()

        w_recv[h, me] = w_send[h]

    def recv_weights(h):
        @pl.loop(1, n_ctx)
        def _(k):
            w_copy(h, k, peer_of(k, n_ctx, me)).wait_recv()

        w_recv[h] = jnp.exp2(top_own[h] - w_recv[h])

    column = lax.broadcasted_iota(jnp.int32, (keys, 128), 1)
    rest = 256 - HEAD_DIM
    scores_refs = (sc0, sc1, sc2, sc3)

    def head_scores(h, p, b):
        a = b % 2
        place = lax.div(p, group)
        start = pl.multiple_of(lax.rem(p, group) * pair_width + a * 128, 128)
        near = k_v[place, :, pl.ds(start, 128)]
        far = k_v[place, :, pl.ds(pl.multiple_of(start + 128, 128), 128)]
        if a == 0:
            far = jnp.where(column < 128 - rest, far, jnp.zeros_like(far))
        else:
            near = jnp.where(column >= rest, near, jnp.zeros_like(near))
        first = h * (row_tiles // 2)
        query = q_v[place, first : first + row_tiles // 2, :, pl.ds(start, 256)]
        scores = matmul_nt(
            jnp.concatenate([near, far], axis=1), query.reshape(lanes_half, 256)
        )
        scores = scores * score_scale + bias[:, h * lanes_half : (h + 1) * lanes_half]
        scores_refs[b][...] = scores
        tops[b] = jnp.max(scores, axis=0, keepdims=True)

    def head_softmax(h, p, b):
        head = 2 * p + b % 2
        top = tops[b]
        expo_head = jnp.exp2(scores_refs[b][...] - top)
        mass = jnp.sum(expo_head, axis=0, keepdims=True)
        probs[head, :, h * lanes_half : (h + 1) * lanes_half] = expo_head.astype(BF16)
        owner = lax.div(head, per_owner) * split
        row = lax.rem(head, per_owner)
        for part in range(split):
            lanes = slice(part * part_rows, (part + 1) * part_rows)
            top_own[h, owner + part, pl.ds(row, 1), :] = top[:, lanes]
            stat_send[h, owner + part, pl.ds(row, 1), :] = mass[:, lanes]

    def wait_group(p):
        k_copy(p).wait()
        for slot in range(SLOTS):
            q_copy(p, slot).wait()

    def attention(h, events):
        if h == 0:
            wait_group(0)
        for b in range(4):
            head_scores(h, b // 2, b)

        @pl.loop(0, pairs // 4)
        def _(i):
            if h == 0:
                pl.when(i + 1 < groups)(lambda: wait_group(i + 1))
            for at, todo in events.items():
                pl.when(i == at)(todo)
            for u in range(2):
                p = 4 * i + 2 * u
                later = jnp.minimum(p + 2, pairs - 2)
                for b in range(4):
                    head_softmax(h, p + b // 2, b)
                    head_scores(h, later + b // 2, b)

        send_stats(h)

    steps = pairs // 4

    def index_softmax(h):
        half = slice(h * lanes_half, (h + 1) * lanes_half)
        for k in range(1, n_head):
            lg_copy(h, k).wait_recv()
        logits = lg_part[h]
        for k in range(1, n_head):
            logits = logits + lg_recv[k - 1, h]
        logits = logits * (LOG2E) + bias[:, half]
        itop = jnp.max(logits, axis=0, keepdims=True)
        logits = jnp.exp2(logits - itop)
        expo[:, half] = logits
        ist_send[h, 0:1, :] = itop
        ist_send[h, 1:2, :] = jnp.sum(logits, axis=0, keepdims=True)

        @pl.loop(1, n_ctx)
        def _(k):
            ist_copy(h, k, me).start()

        ist_recv[h, me] = ist_send[h]

    def index_weights(h):
        @pl.loop(1, n_ctx)
        def _(k):
            peer = peer_of(k, n_ctx, me)
            ist_copy(h, k, peer).wait_recv()

        itops = ist_recv[h, :, 0:1, :]
        imasses = ist_recv[h, :, 1:2, :]
        itop_all = jnp.max(itops, axis=0)
        itotal = jnp.sum(imasses * jnp.exp2(itops - itop_all[None]), axis=0)
        wi_ref[:, h * lanes_half : (h + 1) * lanes_half] = (
            jnp.exp2(ist_send[h, 0:1, :] - itop_all) / itotal
        )

    attention(0, {steps // 4: lambda: ag_forward(1, 0), steps // 2: lambda: ag_forward(0, 0)})
    attention(1, {steps // 4: lambda: ag_forward(0, 1), steps // 2: lambda: ag_forward(1, 1), (3 * steps) // 4: lambda: send_weights(0)})
    index_forward(1)
    index_softmax(0)

    for sub in range(own_tiles):
        first = pl.multiple_of(own_tile(sub) * TILE, TILE)
        own_weights = hw_rows[pl.ds(first, TILE), :]
        for j in range(iheads):
            hwb[sub, j * TILE : (j + 1) * TILE, :] = jnp.broadcast_to(
                own_weights[:, j : j + 1], (TILE, 128)
            )

    for sub in range(own_tiles):
        tile = own_tile(sub)
        for j in range(iheads):
            iqo[sub, j * TILE : (j + 1) * TILE, :] = iq_v[tile, :, j * IDIM : (j + 1) * IDIM]
    qg[...] = jnp.zeros_like(qg)
    kg_part[...] = jnp.zeros_like(kg_part)

    def tg_copy(s, k):
        return head_copy(
            k, tg_part.at[s], tg_recv.at[k - 1, s], tg_s.at[s, k], tg_r.at[s, k]
        )

    def sum_heads(s):
        h, c = s // 2, s % 2
        part, start = c * slot_rows // part_rows, c * slot_rows % part_rows
        lanes = slice(s * slot_rows, (s + 1) * slot_rows)

        def add_owner(o, acc):
            weights = w_recv[h, o * split + part, :, start : start + slot_rows]
            for r in range(per_owner):
                terms = probs[o * per_owner + r, :, lanes]
                acc = acc + terms.astype(F32) * weights[r : r + 1]
            return acc

        tg_part[s] = lax.fori_loop(
            0, n_ctx // split, add_owner, jnp.zeros((keys, slot_rows), F32), unroll=2
        )
        for k in range(1, n_head):
            tg_copy(s, k).start()

    def ps_peer(s, i):
        return lax.div(i * SLOTS + ORDER[s], own_tiles)

    def ps_copy(s, i, peer, slot):
        sub = ORDER[s] % own_tiles
        return pltpu.make_async_remote_copy(
            src_ref=ps_send.at[s, i], dst_ref=ps_recv.at[sub, slot],
            send_sem=ps_s.at[s, i], recv_sem=ps_r.at[sub, slot],
            device_id={"ctx": peer}, device_id_type=MESH,
        )

    def each_peer(s, action):
        @pl.loop(0, spread)
        def _(k):
            i = lax.rem(lax.div(me * own_tiles, SLOTS) + k, spread)
            peer = ps_peer(s, i)

            @pl.when(peer != me)
            def _():
                action(ps_copy(s, i, peer, me))

    def send_step(s):
        for k in range(1, n_head):
            tg_copy(s, k).wait_recv()
        lanes = slice(s * slot_rows, (s + 1) * slot_rows)
        target = tg_part[s]
        for k in range(1, n_head):
            target = target + tg_recv[k - 1, s]
        step = expo[:, lanes] * wi_ref[:, lanes] - target
        pst[:, lanes] = step
        ps_send[s] = step.T.reshape(spread, TILE, keys)
        each_peer(s, lambda copy: copy.start())

    tall = row_tiles // iheads
    wide = group_width // keys

    def sign_place(n, first, width):
        rem = lax.rem(n, tall * wide)
        cols = pl.ds(pl.multiple_of(lax.div(rem, tall) * keys + first, 128), width)
        return (
            lax.div(n, tall * wide),
            pl.ds(lax.rem(rem, tall) * iheads, iheads),
            slice(None),
            cols,
        )

    def query_signs(sub):
        @pl.loop(0, n_ctx // SOURCES)
        def _(g):
            for b in range(SOURCES):
                i = g * SOURCES + b
                source_keys = ikg[peer_of(i, n_ctx, me)].astype(BF16)
                if sub == 0:
                    ikb[i] = source_keys
                act = matmul_nt(iqo[sub], source_keys).astype(BF16)
                q_v[sign_place(sub * n_ctx + i, 0, keys)] = act.reshape(iheads, TILE, keys)

    def key_grad_half(h):
        lanes = slice(h * lanes_half, (h + 1) * lanes_half)

        @pl.loop(0, iheads // batch)
        def _(i):
            terms, queries = [], []
            for b in range(batch):
                j = i * batch + b
                weighted = (pst[:, lanes] * hwt[pl.ds(j, 1), lanes]).astype(BF16)
                terms.append(jnp.where(signs[j, :, lanes] > 0, weighted, jnp.zeros_like(weighted)))
                queries.append(iq_head(j, h))
            kg_part[...] += jnp.dot(
                jnp.concatenate(terms, axis=1),
                jnp.concatenate(queries, axis=0),
                preferred_element_type=F32,
            )

    recv_weights(0)
    sum_heads(0)
    send_weights(1)
    sum_heads(1)
    for stage in range(2, stages - 1):
        for sub in range(2):
            ag_forward(sub, stage)

    index_softmax(1)
    index_weights(0)
    for sub in range(2):
        ag_recv(sub, stages - 1)
    query_signs(0)
    recv_weights(1)
    sum_heads(2)
    send_step(0)
    sum_heads(3)
    send_step(1)
    key_grad_half(0)
    index_weights(1)
    send_step(2)
    send_step(3)
    for sub in range(own_tiles):
        tile = own_tile(sub)
        ps_recv[sub, me] = ps_send[lax.div(tile, spread), lax.rem(tile, spread)]
    key_grad_half(1)

    def kg_copy(k):
        return head_copy(k, kg_part, kg_recv.at[k - 1], kg_s.at[k], kg_r.at[k])

    for k in range(1, n_head):
        kg_copy(k).start()

    for sub in range(1, own_tiles):
        query_signs(sub)

    def source_terms(sub, i, source):
        terms = []
        for c in range(keys // 128):
            lanes = slice(c * 128, (c + 1) * 128)
            step = ps_recv[sub, source, :, lanes]
            weighted = (hwb[sub].reshape(iheads, TILE, 128) * step[None]).astype(BF16)
            act = q_v[sign_place(sub * n_ctx + i, c * 128, 128)]
            terms.append(
                jnp.where(act > 0, weighted, jnp.zeros_like(weighted)).reshape(-1, 128)
            )
        return terms

    for sub in range(own_tiles):
        @pl.loop(1, n_ctx)
        def _(k):
            source = peer_of(k, n_ctx, me)
            ps_copy(ORDER.index(sub), 0, source, source).wait_recv()

        @pl.loop(0, n_ctx // SOURCES)
        def _(g):
            terms, source_keys = [], []
            for b in range(SOURCES):
                i = g * SOURCES + b
                terms += source_terms(sub, i, peer_of(i, n_ctx, me))
                source_keys.append(ikb[i])
            qg[sub] += jnp.dot(
                jnp.concatenate(terms, axis=1),
                jnp.concatenate(source_keys, axis=0),
                preferred_element_type=F32,
            )

    for sub in range(own_tiles):
        for j in range(iheads):
            qgrad_ref[sub * TILE : (sub + 1) * TILE, j * IDIM : (j + 1) * IDIM] = qg[
                sub, j * TILE : (j + 1) * TILE, :
            ]

    key_grad = kg_part[...]
    for k in range(1, n_head):
        kg_copy(k).wait_recv()
        key_grad = key_grad + kg_recv[k - 1]
    kgrad_ref[...] = key_grad

    for s in range(stages):
        for sub in range(2):
            ag_sent(sub, s)
    for k in range(1, n_head):
        for h in range(2):
            lg_copy(h, k).wait_send()
        kg_copy(k).wait_send()
        for s in range(SLOTS):
            tg_copy(s, k).wait_send()

    @pl.loop(1, n_ctx)
    def _(k):
        peer = peer_of(k, n_ctx, me)
        for h in range(2):
            ist_copy(h, k, me).wait_send()
            stat_copy(h, k, peer, me).wait_send()
            w_copy(h, k, me).wait_send()

    for s in range(SLOTS):
        each_peer(s, lambda copy: copy.wait_send())


def hand_on(query_ref, key_ref, query_out, key_out):
    query_out[...] = query_ref[...]
    key_out[...] = key_ref[...]


def shards(n_ctx, n_head, queries, attn_keys, index_queries, index_keys, head_weights, query_pos, key_offset):
    rows = queries.shape[0]
    keys = attn_keys.shape[0]
    heads = attn_keys.shape[1] // HEAD_DIM
    iheads = index_queries.shape[1] // IDIM
    own_tiles = rows // n_ctx // TILE
    row_tiles = rows // TILE
    spread = row_tiles // SLOTS
    slot_rows = rows // SLOTS
    group = math.gcd(GROUP, heads // 2)
    groups = heads // 2 // group
    per_owner = max(1, heads // n_ctx)
    split = n_ctx * per_owner // heads
    stages = n_ctx.bit_length() - 1
    vmem = pltpu.VMEM
    dma = pltpu.SemaphoreType.DMA
    any_space = pl.BlockSpec(memory_space=pl.ANY)
    vmem_space = pl.BlockSpec(memory_space=pltpu.VMEM)
    query_grad, key_grad = pl.pallas_call(
        functools.partial(kernel, n_ctx, n_head, heads),
        out_shape=(
            jax.ShapeDtypeStruct((rows // n_ctx, iheads * IDIM), F32),
            jax.ShapeDtypeStruct((keys, IDIM), F32),
        ),
        in_specs=[any_space] * 3 + [vmem_space] * 4,
        out_specs=(vmem_space, vmem_space),
        scratch_shapes=[
            vmem((groups, row_tiles, TILE, 2 * HEAD_DIM * group), BF16),
            vmem((groups, keys, 2 * HEAD_DIM * group), BF16),
            vmem((row_tiles, TILE, iheads * IDIM), BF16),
            vmem((heads, keys, rows), BF16),
            vmem((n_ctx, keys, IDIM), F32),
            vmem((keys, rows), F32),
            vmem((2, keys, rows // 2), F32),
            vmem((n_head - 1, 2, keys, rows // 2), F32),
            vmem((keys, rows), F32),
            vmem((2, n_ctx, per_owner, rows // 2 // split), F32),
            vmem((2, n_ctx, per_owner, rows // 2 // split), F32),
            vmem((2, n_ctx, per_owner, rows // 2 // split), F32),
            vmem((2, 2, rows // 2), F32),
            vmem((2, n_ctx, 2, rows // 2), F32),
            vmem((2, per_owner, rows // 2 // split), F32),
            vmem((2, n_ctx, per_owner, rows // 2 // split), F32),
            vmem((1, rows), F32),
            vmem((SLOTS, keys, slot_rows), F32),
            vmem((n_head - 1, SLOTS, keys, slot_rows), F32),
            vmem((keys, rows), F32),
            vmem((SLOTS, spread, TILE, keys), F32),
            vmem((own_tiles, n_ctx, TILE, keys), F32),
            vmem((keys, IDIM), F32),
            vmem((n_head - 1, keys, IDIM), F32),
            vmem((own_tiles, iheads * TILE, IDIM), F32),
            vmem((own_tiles, iheads * TILE, 128), F32),
            vmem((rows, 128), F32),
            vmem((iheads, rows), F32),
            vmem((own_tiles, iheads * TILE, IDIM), BF16),
            *[vmem((keys, rows // 2), F32)] * 4,
            vmem((4, 1, rows // 2), F32),
            vmem((iheads, keys, rows), BF16),
            vmem((n_ctx, keys, IDIM), BF16),
            dma((groups, SLOTS)),
            dma((groups,)),
            dma((SLOTS,)),
            dma((stages, 2, n_ctx)),
            dma((2, n_ctx)),
            dma((2, n_head)),
            dma((2, n_head)),
            dma((2, n_ctx)),
            dma((2, n_ctx)),
            dma((2, n_ctx)),
            dma((2, n_ctx)),
            dma((2, n_ctx)),
            dma((2, n_ctx)),
            dma((SLOTS, n_head)),
            dma((SLOTS, n_head)),
            dma((SLOTS, spread)),
            dma((own_tiles, n_ctx)),
            dma((n_head,)),
            dma((n_head,)),
        ],
        compiler_params=pltpu.CompilerParams(
            collective_id=0, has_side_effects=True, vmem_limit_bytes=64 * 1024 * 1024 - 65536
        ),
    )(
        queries.reshape(spread, SLOTS, TILE, queries.shape[1]),
        attn_keys,
        index_queries.reshape(spread, SLOTS, TILE, index_queries.shape[1]),
        index_keys,
        head_weights.T,
        query_pos.reshape(1, rows),
        key_offset.reshape(1, keys),
    )
    return pl.pallas_call(
        hand_on,
        out_shape=(
            jax.ShapeDtypeStruct(query_grad.shape, F32),
            jax.ShapeDtypeStruct(key_grad.shape, F32),
        ),
        in_specs=[vmem_space] * 2,
        out_specs=(vmem_space, vmem_space),
    )(query_grad, key_grad)


def solution(mesh):
    in_specs = (
        P(None, "head"),
        P("ctx", "head"),
        P(None, "head"),
        P("ctx", None),
        P(None, "head"),
        P(),
        P("ctx"),
    )
    out_specs = (P("ctx", "head"), P("ctx", None))
    body = functools.partial(shards, mesh.shape["ctx"], mesh.shape["head"])
    return jax.shard_map(body, mesh=mesh, in_specs=in_specs, out_specs=out_specs, check_vma=False)
```

```python
import functools
import math

import jax
import jax.numpy as jnp
from jax import lax
from jax.experimental import pallas as pl
from jax.experimental.pallas import tpu as pltpu
from jax.sharding import PartitionSpec as P

HEADS = 128
HEAD_DIM = 192
IDIM = 128
STRIDE = 8
NEG_FILL = -1e30
LOG2E = math.log2(math.e)
GROUP = 4
PAIRS = 8
BATCH = 8
SOURCES = 4
TILE = 16
SLOTS = 4
ORDER = (0, 2, 1, 3)
MESH = pl.DeviceIdType.MESH
F32 = jnp.float32
BF16 = jnp.bfloat16
NT = (((1,), (1,)), ((), ()))


def matmul_nt(a, b):
    return lax.dot_general(a, b, NT, preferred_element_type=F32)


def kernel(
    n_ctx, n_head, heads,
    q_hbm, k_hbm, iq_hbm, ik_ref, hwt_ref, qpos_ref, koff_ref,
    qgrad_ref, kgrad_ref,
    q_v, k_v, iq_v, probs, ikg, bias, lg_part, lg_recv, expo,
    stat_send, stat_recv, top_own, ist_send, ist_recv, w_send, w_recv, wi_ref,
    tg_part, tg_recv, pst, ps_send, ps_recv, kg_part, kg_recv, qg, hwb, hw_rows, hwt, iqo,
    sc0, sc1, sc2, sc3, tops, signs, ikb,
    q_sem, k_sem, iq_sem, ag_s, ag_r, lg_s, lg_r, st_s, st_r, is_s, is_r,
    w_s, w_r, tg_s, tg_r, ps_s, ps_r, kg_s, kg_r,
):
    me = lax.axis_index("ctx")
    my_head = lax.axis_index("head")
    groups, row_tiles, _, group_width = q_v.shape
    rows = row_tiles * TILE
    pair_width = 2 * HEAD_DIM
    group = group_width // pair_width
    pairs = groups * group
    keys = k_v.shape[1]
    iheads = iq_v.shape[2] // IDIM
    own = rows // n_ctx
    own_tiles = own // TILE
    spread = row_tiles // SLOTS
    slot_rows = rows // SLOTS
    per_owner = max(1, 2 * pairs // n_ctx)
    split = n_ctx * per_owner // (2 * pairs)
    lanes_half = rows // 2
    part_rows = lanes_half // split
    score_scale = LOG2E / math.sqrt(HEAD_DIM)
    inv_scale = 1.0 / math.sqrt(IDIM)

    def peer_of(k, n, base):
        return lax.rem(base + k, n)

    def q_copy(p, slot):
        cols = pl.ds(pl.multiple_of(p * group_width, 128), group_width)
        return pltpu.make_async_copy(
            q_hbm.at[:, ORDER[slot], :, cols],
            q_v.at[p, pl.ds(slot * spread, spread)],
            q_sem.at[p, slot],
        )

    def k_copy(p):
        cols = pl.ds(pl.multiple_of(p * group_width, 128), group_width)
        return pltpu.make_async_copy(k_hbm.at[:, cols], k_v.at[p], k_sem.at[p])

    def iq_copy(slot):
        return pltpu.make_async_copy(
            iq_hbm.at[:, ORDER[slot]], iq_v.at[pl.ds(slot * spread, spread)], iq_sem.at[slot]
        )

    def iq_head(j, half):
        cols = pl.ds(pl.multiple_of(j * IDIM, 128), IDIM)
        first = half * (row_tiles // 2)
        return iq_v[first : first + row_tiles // 2, :, cols].reshape(lanes_half, IDIM)

    for slot in range(SLOTS):
        iq_copy(slot).start()

    @pl.loop(0, groups)
    def _(p):
        k_copy(p).start()
        for slot in range(SLOTS):
            q_copy(p, slot).start()

    barrier = pltpu.get_barrier_semaphore()
    for k in range(1, n_ctx):
        pl.semaphore_signal(
            barrier, inc=1, device_id={"ctx": peer_of(k, n_ctx, me)}, device_id_type=MESH
        )
    for k in range(1, n_head):
        pl.semaphore_signal(
            barrier, inc=1, device_id={"head": peer_of(k, n_head, my_head)}, device_id_type=MESH
        )

    ikg[me] = ik_ref[...].astype(F32)
    offset = jnp.broadcast_to(koff_ref[...].astype(F32), (128, keys)).T[:, 0:1].astype(jnp.int32)
    key_pos = STRIDE * (me * keys + lax.broadcasted_iota(jnp.int32, (keys, 1), 0)) + offset
    by_query = jnp.concatenate(
        [
            hwt_ref[...] * inv_scale,
            jnp.broadcast_to(qpos_ref[...].astype(F32), (128 - iheads, rows)),
        ],
        axis=0,
    ).T.reshape(spread, SLOTS, TILE, 128)
    by_query = jnp.concatenate(
        [by_query[:, ORDER[slot]].reshape(slot_rows, 128) for slot in range(SLOTS)], axis=0
    )
    hw_rows[...] = by_query
    by_lane = by_query.T
    hwt[...] = by_lane[:iheads]
    query_pos = by_lane[127:128].astype(jnp.int32)
    bias[...] = jnp.where(key_pos <= query_pos, 0.0, NEG_FILL)

    def own_tile(sub):
        tile = me * own_tiles + sub
        m = lax.rem(tile, SLOTS)
        return (lax.rem(m, 2) * 2 + lax.div(m, 2)) * spread + lax.div(tile, SLOTS)

    pl.semaphore_wait(barrier, n_ctx - 1 + n_head - 1)

    bits = [1 << b for b in reversed(range(n_ctx.bit_length() - 1))]
    stages = len(bits)
    turn = stages // 2
    orders = (bits, bits[turn:-1] + bits[:turn] + bits[-1:])

    def flip(index, bit):
        return index + bit * (1 - 2 * lax.rem(lax.div(index, bit), 2))

    def ag_shards(sub, stage, base):
        shards = [base]
        for bit in orders[sub][:stage]:
            shards = shards + [flip(s, bit) for s in shards]
        return shards

    sub_rows = keys // 2

    def ag_copy(shard, sub, stage):
        piece = ikg.at[shard, pl.ds(sub * sub_rows, sub_rows)]
        return pltpu.make_async_remote_copy(
            src_ref=piece, dst_ref=piece,
            send_sem=ag_s.at[stage, sub, shard], recv_sem=ag_r.at[sub, shard],
            device_id={"ctx": flip(me, orders[sub][stage])}, device_id_type=MESH,
        )

    def ag_start(sub, stage):
        for shard in ag_shards(sub, stage, me):
            ag_copy(shard, sub, stage).start()

    def ag_recv(sub, stage):
        for shard in ag_shards(sub, stage, flip(me, orders[sub][stage])):
            ag_copy(shard, sub, stage).wait_recv()

    def ag_sent(sub, stage):
        for shard in ag_shards(sub, stage, me):
            ag_copy(shard, sub, stage).wait_send()

    def ag_forward(sub, stage):
        ag_recv(sub, stage)
        ag_start(sub, stage + 1)

    for sub in range(2):
        ag_start(sub, 0)

    for slot in range(SLOTS):
        iq_copy(slot).wait()

    batch = math.gcd(BATCH, iheads)

    def index_forward(h):
        half = slice(h * lanes_half, (h + 1) * lanes_half)
        lg_part[h] = jnp.zeros_like(lg_part[h])

        @pl.loop(0, iheads // batch)
        def _(i):
            total = None
            for b in range(batch):
                j = i * batch + b
                act = matmul_nt(ik_ref[...], iq_head(j, h))
                signs[j, :, half] = act.astype(BF16)
                term = hwt[pl.ds(j, 1), half] * jnp.maximum(act, 0.0)
                total = term if total is None else total + term
            lg_part[h] += total

        for k in range(1, n_head):
            lg_copy(h, k).start()

    def head_copy(k, src, dst, send, recv):
        return pltpu.make_async_remote_copy(
            src_ref=src, dst_ref=dst, send_sem=send, recv_sem=recv,
            device_id={"head": peer_of(k, n_head, my_head)}, device_id_type=MESH,
        )

    def lg_copy(h, k):
        return head_copy(k, lg_part.at[h], lg_recv.at[k - 1, h], lg_s.at[h, k], lg_r.at[h, k])

    index_forward(0)

    def ctx_copy(k, src, dst, send, recv):
        return pltpu.make_async_remote_copy(
            src_ref=src, dst_ref=dst, send_sem=send, recv_sem=recv,
            device_id={"ctx": peer_of(k, n_ctx, me)}, device_id_type=MESH,
        )

    def stat_copy(h, k, peer, slot):
        return ctx_copy(
            k, stat_send.at[h, peer], stat_recv.at[h, slot], st_s.at[h, k], st_r.at[h, slot]
        )

    def ist_copy(h, k, slot):
        return ctx_copy(k, ist_send.at[h], ist_recv.at[h, slot], is_s.at[h, k], is_r.at[h, slot])

    def w_copy(h, k, slot):
        return ctx_copy(k, w_send.at[h], w_recv.at[h, slot], w_s.at[h, k], w_r.at[h, slot])

    def send_stats(h):
        stat_send[h] = top_own[h] + jnp.log2(stat_send[h])

        @pl.loop(1, n_ctx)
        def _(k):
            stat_copy(h, k, peer_of(k, n_ctx, me), me).start()

        stat_recv[h, me] = stat_send[h, me]

    def send_weights(h):
        @pl.loop(1, n_ctx)
        def _(k):
            peer = peer_of(k, n_ctx, me)
            stat_copy(h, k, peer, peer).wait_recv()

        levels = stat_recv[h]
        top = jnp.max(levels, axis=0)
        total = jnp.sum(jnp.exp2(levels - top[None]), axis=0)
        w_send[h] = top + jnp.log2(HEADS * total)

        @pl.loop(1, n_ctx)
        def _(k):
            w_copy(h, k, me).start()

        w_recv[h, me] = w_send[h]

    def recv_weights(h):
        @pl.loop(1, n_ctx)
        def _(k):
            w_copy(h, k, peer_of(k, n_ctx, me)).wait_recv()

        w_recv[h] = jnp.exp2(top_own[h] - w_recv[h])

    column = lax.broadcasted_iota(jnp.int32, (keys, 128), 1)
    rest = 256 - HEAD_DIM
    scores_refs = (sc0, sc1, sc2, sc3)

    def head_scores(h, p, b):
        a = b % 2
        place = lax.div(p, group)
        start = pl.multiple_of(lax.rem(p, group) * pair_width + a * 128, 128)
        near = k_v[place, :, pl.ds(start, 128)]
        far = k_v[place, :, pl.ds(pl.multiple_of(start + 128, 128), 128)]
        if a == 0:
            far = jnp.where(column < 128 - rest, far, jnp.zeros_like(far))
        else:
            near = jnp.where(column >= rest, near, jnp.zeros_like(near))
        first = h * (row_tiles // 2)
        query = q_v[place, first : first + row_tiles // 2, :, pl.ds(start, 256)]
        scores = matmul_nt(
            jnp.concatenate([near, far], axis=1), query.reshape(lanes_half, 256)
        )
        scores = scores * score_scale + bias[:, h * lanes_half : (h + 1) * lanes_half]
        scores_refs[b][...] = scores
        tops[b] = jnp.max(scores, axis=0, keepdims=True)

    def head_softmax(h, p, b):
        head = 2 * p + b % 2
        top = tops[b]
        expo_head = jnp.exp2(scores_refs[b][...] - top)
        mass = jnp.sum(expo_head, axis=0, keepdims=True)
        probs[head, :, h * lanes_half : (h + 1) * lanes_half] = expo_head.astype(BF16)
        owner = lax.div(head, per_owner) * split
        row = lax.rem(head, per_owner)
        for part in range(split):
            lanes = slice(part * part_rows, (part + 1) * part_rows)
            top_own[h, owner + part, pl.ds(row, 1), :] = top[:, lanes]
            stat_send[h, owner + part, pl.ds(row, 1), :] = mass[:, lanes]

    def wait_group(p):
        k_copy(p).wait()
        for slot in range(SLOTS):
            q_copy(p, slot).wait()

    step_pairs = max(group, math.gcd(PAIRS, pairs))
    steps = pairs // step_pairs

    def attention(h, events):
        if h == 0:
            wait_group(0)
        for b in range(4):
            head_scores(h, b // 2, b)

        @pl.loop(0, steps)
        def _(i):
            if h == 0:
                for g in range(1, step_pairs // group + 1):
                    place = i * (step_pairs // group) + g
                    pl.when(place < groups)(functools.partial(wait_group, place))
            for at, todo in events:
                pl.when(i == at)(todo)
            for u in range(step_pairs // 2):
                p = step_pairs * i + 2 * u
                later = jnp.minimum(p + 2, pairs - 2)
                for b in range(4):
                    head_softmax(h, p + b // 2, b)
                    head_scores(h, later + b // 2, b)

        send_stats(h)


    def index_softmax(h):
        half = slice(h * lanes_half, (h + 1) * lanes_half)
        for k in range(1, n_head):
            lg_copy(h, k).wait_recv()
        logits = lg_part[h]
        for k in range(1, n_head):
            logits = logits + lg_recv[k - 1, h]
        logits = logits * (LOG2E) + bias[:, half]
        itop = jnp.max(logits, axis=0, keepdims=True)
        logits = jnp.exp2(logits - itop)
        expo[:, half] = logits
        ist_send[h, 0:1, :] = itop
        ist_send[h, 1:2, :] = jnp.sum(logits, axis=0, keepdims=True)

        @pl.loop(1, n_ctx)
        def _(k):
            ist_copy(h, k, me).start()

        ist_recv[h, me] = ist_send[h]

    def index_weights(h):
        @pl.loop(1, n_ctx)
        def _(k):
            peer = peer_of(k, n_ctx, me)
            ist_copy(h, k, peer).wait_recv()

        itops = ist_recv[h, :, 0:1, :]
        imasses = ist_recv[h, :, 1:2, :]
        itop_all = jnp.max(itops, axis=0)
        itotal = jnp.sum(imasses * jnp.exp2(itops - itop_all[None]), axis=0)
        wi_ref[:, h * lanes_half : (h + 1) * lanes_half] = (
            jnp.exp2(ist_send[h, 0:1, :] - itop_all) / itotal
        )

    attention(0, [(steps // 4, lambda: ag_forward(1, 0)), (steps // 2, lambda: ag_forward(0, 0))])
    attention(
        1,
        [
            (steps // 4, lambda: ag_forward(0, 1)),
            (steps // 2, lambda: ag_forward(1, 1)),
            ((3 * steps) // 4, lambda: send_weights(0)),
        ],
    )
    index_forward(1)
    index_softmax(0)

    for sub in range(own_tiles):
        first = pl.multiple_of(own_tile(sub) * TILE, TILE)
        own_weights = hw_rows[pl.ds(first, TILE), :]
        for j in range(iheads):
            hwb[sub, j * TILE : (j + 1) * TILE, :] = jnp.broadcast_to(
                own_weights[:, j : j + 1], (TILE, 128)
            )

    for sub in range(own_tiles):
        tile = own_tile(sub)
        for j in range(iheads):
            iqo[sub, j * TILE : (j + 1) * TILE, :] = iq_v[tile, :, j * IDIM : (j + 1) * IDIM]
    qg[...] = jnp.zeros_like(qg)
    kg_part[...] = jnp.zeros_like(kg_part)

    def tg_copy(s, k):
        return head_copy(
            k, tg_part.at[s], tg_recv.at[k - 1, s], tg_s.at[s, k], tg_r.at[s, k]
        )

    def sum_heads(s):
        h, c = s // 2, s % 2
        part, start = c * slot_rows // part_rows, c * slot_rows % part_rows
        lanes = slice(s * slot_rows, (s + 1) * slot_rows)

        def add_owner(o, acc):
            weights = w_recv[h, o * split + part, :, start : start + slot_rows]
            for r in range(per_owner):
                terms = probs[o * per_owner + r, :, lanes]
                acc = acc + terms.astype(F32) * weights[r : r + 1]
            return acc

        tg_part[s] = lax.fori_loop(
            0, n_ctx // split, add_owner, jnp.zeros((keys, slot_rows), F32), unroll=4
        )
        for k in range(1, n_head):
            tg_copy(s, k).start()

    def ps_peer(s, i):
        return lax.div(i * SLOTS + ORDER[s], own_tiles)

    def ps_copy(s, i, peer, slot):
        sub = ORDER[s] % own_tiles
        return pltpu.make_async_remote_copy(
            src_ref=ps_send.at[s, i], dst_ref=ps_recv.at[sub, slot],
            send_sem=ps_s.at[s, i], recv_sem=ps_r.at[sub, slot],
            device_id={"ctx": peer}, device_id_type=MESH,
        )

    def each_peer(s, action):
        @pl.loop(0, spread)
        def _(k):
            i = lax.rem(lax.div(me * own_tiles, SLOTS) + k, spread)
            peer = ps_peer(s, i)

            @pl.when(peer != me)
            def _():
                action(ps_copy(s, i, peer, me))

    def send_step(s):
        for k in range(1, n_head):
            tg_copy(s, k).wait_recv()
        lanes = slice(s * slot_rows, (s + 1) * slot_rows)
        target = tg_part[s]
        for k in range(1, n_head):
            target = target + tg_recv[k - 1, s]
        step = expo[:, lanes] * wi_ref[:, lanes] - target
        pst[:, lanes] = step
        ps_send[s] = step.T.reshape(spread, TILE, keys)
        each_peer(s, lambda copy: copy.start())

    tall = row_tiles // iheads
    wide = group_width // keys

    def sign_place(n, first, width):
        rem = lax.rem(n, tall * wide)
        cols = pl.ds(pl.multiple_of(lax.div(rem, tall) * keys + first, 128), width)
        return (
            lax.div(n, tall * wide),
            pl.ds(lax.rem(rem, tall) * iheads, iheads),
            slice(None),
            cols,
        )

    def query_signs(sub):
        @pl.loop(0, n_ctx // SOURCES)
        def _(g):
            for b in range(SOURCES):
                i = g * SOURCES + b
                source_keys = ikg[peer_of(i, n_ctx, me)].astype(BF16)
                if sub == 0:
                    ikb[i] = source_keys
                act = matmul_nt(iqo[sub], source_keys).astype(BF16)
                q_v[sign_place(sub * n_ctx + i, 0, keys)] = act.reshape(iheads, TILE, keys)

    def key_grad_half(h):
        lanes = slice(h * lanes_half, (h + 1) * lanes_half)

        @pl.loop(0, iheads // batch)
        def _(i):
            terms, queries = [], []
            for b in range(batch):
                j = i * batch + b
                weighted = (pst[:, lanes] * hwt[pl.ds(j, 1), lanes]).astype(BF16)
                terms.append(jnp.where(signs[j, :, lanes] > 0, weighted, jnp.zeros_like(weighted)))
                queries.append(iq_head(j, h))
            kg_part[...] += jnp.dot(
                jnp.concatenate(terms, axis=1),
                jnp.concatenate(queries, axis=0),
                preferred_element_type=F32,
            )

    recv_weights(0)
    sum_heads(0)
    send_weights(1)
    sum_heads(1)
    for stage in range(2, stages - 1):
        for sub in range(2):
            ag_forward(sub, stage)

    index_softmax(1)
    index_weights(0)
    recv_weights(1)
    sum_heads(2)
    send_step(0)
    sum_heads(3)
    send_step(1)
    key_grad_half(0)
    for sub in range(2):
        ag_recv(sub, stages - 1)
    query_signs(0)
    index_weights(1)
    send_step(2)
    send_step(3)
    for sub in range(own_tiles):
        tile = own_tile(sub)
        ps_recv[sub, me] = ps_send[lax.div(tile, spread), lax.rem(tile, spread)]
    key_grad_half(1)

    def kg_copy(k):
        return head_copy(k, kg_part, kg_recv.at[k - 1], kg_s.at[k], kg_r.at[k])

    for k in range(1, n_head):
        kg_copy(k).start()

    for sub in range(1, own_tiles):
        query_signs(sub)

    def source_terms(sub, i, source):
        terms = []
        for c in range(keys // 128):
            lanes = slice(c * 128, (c + 1) * 128)
            step = ps_recv[sub, source, :, lanes]
            weighted = (hwb[sub].reshape(iheads, TILE, 128) * step[None]).astype(BF16)
            act = q_v[sign_place(sub * n_ctx + i, c * 128, 128)]
            terms.append(
                jnp.where(act > 0, weighted, jnp.zeros_like(weighted)).reshape(-1, 128)
            )
        return terms

    for sub in range(own_tiles):
        @pl.loop(1, n_ctx)
        def _(k):
            source = peer_of(k, n_ctx, me)
            ps_copy(ORDER.index(sub), 0, source, source).wait_recv()

        @pl.loop(0, n_ctx // SOURCES)
        def _(g):
            terms, source_keys = [], []
            for b in range(SOURCES):
                i = g * SOURCES + b
                terms += source_terms(sub, i, peer_of(i, n_ctx, me))
                source_keys.append(ikb[i])
            qg[sub] += jnp.dot(
                jnp.concatenate(terms, axis=1),
                jnp.concatenate(source_keys, axis=0),
                preferred_element_type=F32,
            )

    for sub in range(own_tiles):
        for j in range(iheads):
            qgrad_ref[sub * TILE : (sub + 1) * TILE, j * IDIM : (j + 1) * IDIM] = qg[
                sub, j * TILE : (j + 1) * TILE, :
            ]

    key_grad = kg_part[...]
    for k in range(1, n_head):
        kg_copy(k).wait_recv()
        key_grad = key_grad + kg_recv[k - 1]
    kgrad_ref[...] = key_grad

    for s in range(stages):
        for sub in range(2):
            ag_sent(sub, s)
    for k in range(1, n_head):
        for h in range(2):
            lg_copy(h, k).wait_send()
        kg_copy(k).wait_send()
        for s in range(SLOTS):
            tg_copy(s, k).wait_send()

    @pl.loop(1, n_ctx)
    def _(k):
        peer = peer_of(k, n_ctx, me)
        for h in range(2):
            ist_copy(h, k, me).wait_send()
            stat_copy(h, k, peer, me).wait_send()
            w_copy(h, k, me).wait_send()

    for s in range(SLOTS):
        each_peer(s, lambda copy: copy.wait_send())


def hand_on(query_ref, key_ref, query_out, key_out):
    query_out[...] = query_ref[...]
    key_out[...] = key_ref[...]


def shards(n_ctx, n_head, queries, attn_keys, index_queries, index_keys, head_weights, query_pos, key_offset):
    rows = queries.shape[0]
    keys = attn_keys.shape[0]
    heads = attn_keys.shape[1] // HEAD_DIM
    iheads = index_queries.shape[1] // IDIM
    own_tiles = rows // n_ctx // TILE
    row_tiles = rows // TILE
    spread = row_tiles // SLOTS
    slot_rows = rows // SLOTS
    group = math.gcd(GROUP, heads // 2)
    groups = heads // 2 // group
    per_owner = max(1, heads // n_ctx)
    split = n_ctx * per_owner // heads
    stages = n_ctx.bit_length() - 1
    vmem = pltpu.VMEM
    dma = pltpu.SemaphoreType.DMA
    any_space = pl.BlockSpec(memory_space=pl.ANY)
    vmem_space = pl.BlockSpec(memory_space=pltpu.VMEM)
    query_grad, key_grad = pl.pallas_call(
        functools.partial(kernel, n_ctx, n_head, heads),
        out_shape=(
            jax.ShapeDtypeStruct((rows // n_ctx, iheads * IDIM), F32),
            jax.ShapeDtypeStruct((keys, IDIM), F32),
        ),
        in_specs=[any_space] * 3 + [vmem_space] * 4,
        out_specs=(vmem_space, vmem_space),
        scratch_shapes=[
            vmem((groups, row_tiles, TILE, 2 * HEAD_DIM * group), BF16),
            vmem((groups, keys, 2 * HEAD_DIM * group), BF16),
            vmem((row_tiles, TILE, iheads * IDIM), BF16),
            vmem((heads, keys, rows), BF16),
            vmem((n_ctx, keys, IDIM), F32),
            vmem((keys, rows), F32),
            vmem((2, keys, rows // 2), F32),
            vmem((n_head - 1, 2, keys, rows // 2), F32),
            vmem((keys, rows), F32),
            vmem((2, n_ctx, per_owner, rows // 2 // split), F32),
            vmem((2, n_ctx, per_owner, rows // 2 // split), F32),
            vmem((2, n_ctx, per_owner, rows // 2 // split), F32),
            vmem((2, 2, rows // 2), F32),
            vmem((2, n_ctx, 2, rows // 2), F32),
            vmem((2, per_owner, rows // 2 // split), F32),
            vmem((2, n_ctx, per_owner, rows // 2 // split), F32),
            vmem((1, rows), F32),
            vmem((SLOTS, keys, slot_rows), F32),
            vmem((n_head - 1, SLOTS, keys, slot_rows), F32),
            vmem((keys, rows), F32),
            vmem((SLOTS, spread, TILE, keys), F32),
            vmem((own_tiles, n_ctx, TILE, keys), F32),
            vmem((keys, IDIM), F32),
            vmem((n_head - 1, keys, IDIM), F32),
            vmem((own_tiles, iheads * TILE, IDIM), F32),
            vmem((own_tiles, iheads * TILE, 128), F32),
            vmem((rows, 128), F32),
            vmem((iheads, rows), F32),
            vmem((own_tiles, iheads * TILE, IDIM), BF16),
            *[vmem((keys, rows // 2), F32)] * 4,
            vmem((4, 1, rows // 2), F32),
            vmem((iheads, keys, rows), BF16),
            vmem((n_ctx, keys, IDIM), BF16),
            dma((groups, SLOTS)),
            dma((groups,)),
            dma((SLOTS,)),
            dma((stages, 2, n_ctx)),
            dma((2, n_ctx)),
            dma((2, n_head)),
            dma((2, n_head)),
            dma((2, n_ctx)),
            dma((2, n_ctx)),
            dma((2, n_ctx)),
            dma((2, n_ctx)),
            dma((2, n_ctx)),
            dma((2, n_ctx)),
            dma((SLOTS, n_head)),
            dma((SLOTS, n_head)),
            dma((SLOTS, spread)),
            dma((own_tiles, n_ctx)),
            dma((n_head,)),
            dma((n_head,)),
        ],
        compiler_params=pltpu.CompilerParams(
            collective_id=0, has_side_effects=True, vmem_limit_bytes=64 * 1024 * 1024 - 65536
        ),
    )(
        queries.reshape(spread, SLOTS, TILE, queries.shape[1]),
        attn_keys,
        index_queries.reshape(spread, SLOTS, TILE, index_queries.shape[1]),
        index_keys,
        head_weights.T,
        query_pos.reshape(1, rows),
        key_offset.reshape(1, keys),
    )
    return pl.pallas_call(
        hand_on,
        out_shape=(
            jax.ShapeDtypeStruct(query_grad.shape, F32),
            jax.ShapeDtypeStruct(key_grad.shape, F32),
        ),
        in_specs=[vmem_space] * 2,
        out_specs=(vmem_space, vmem_space),
    )(query_grad, key_grad)


def solution(mesh):
    in_specs = (
        P(None, "head"),
        P("ctx", "head"),
        P(None, "head"),
        P("ctx", None),
        P(None, "head"),
        P(),
        P("ctx"),
    )
    out_specs = (P("ctx", "head"), P("ctx", None))
    body = functools.partial(shards, mesh.shape["ctx"], mesh.shape["head"])
    return jax.shard_map(body, mesh=mesh, in_specs=in_specs, out_specs=out_specs, check_vma=False)
```
